32 devices in a mesh: gx: 16 (over z, y, x), gy: 2 (over core).
Axes of the slice: x: 2, y: 2, z: 4, core: 2. Of those that a mesh axis runs over, the one named last changes fastest.
Arguments:
- coarse_state: float32 [24, 256, 256], P(None, 'gx', 'gy'), may hold values from -6 to 6
- coarse_rate: float32 [256, 256], P('gx', 'gy'), may hold values from 0.5 to 2
- fine_state: float32 [128, 24, 16, 256], P(('gx', 'gy')), may hold values from -6 to 6
- fine_rate: float32 [128, 16, 256], P(('gx', 'gy')), may hold values from 0.5 to 2
- refine_to: int32 [128], P(('gx', 'gy')), may hold values from -1 to 3, as said below
- parent_of: int32 [128], P(('gx', 'gy')), may hold values from -1 to 3, as said below
- kappa: float32 [24], replicated, may hold values from 0.01 to 0.05
- reaction: float32 [24, 24], replicated, may hold values from -1.25 to 1.25
Outputs:
- coarse_out: float32 [24, 256, 256], P(None, 'gx', 'gy')
- fine_out: float32 [128, 24, 16, 256], P(('gx', 'gy'))
The draws below stay inside these ranges and needn't reach their ends.
Inputs may be any that keep to these rules, and one draw needn't show every extreme that they name: `refine_to`: -1 for a parent that is not refined; else k, the slot of its fine patch on the device k // 2 places higher along gx (wrapping), same gy index; no two parents name the same slot. `parent_of`: -1 for an empty slot; else p, its parent on the device k // 2 places lower along gx (wrapping), same gy index, k being the slot within its device; the two maps are inverse to each other; a device holds up to 4 live slots and in every draw some device holds that many.
All inputs are finite; a program needn't handle non-finite values.
Results may differ from the reference program's by a relative error of at most 0.0003.
Values sent between devices are 32-bit elements; how exact they have to be, the bound alone decides.
A program may use at most 64 MiB of HBM per device.

```python
import math
import jax
import jax.numpy as jnp
from jax import lax

F = 24
CX = 16
CY = 16
NZ = 8
REACH = 2
PAR_DEV = 4
SUBSTEPS = 4
NX = 256
NY = 32
FZ = 16
PARENTS = 128
SLOT_DEV = 4
SLOTS = 128
N_GX = 16
N_GY = 2
DEVICES = 32


def build_maps(key):
    base_key = jax.random.fold_in(key, 11)
    key_busy, key_pick, key_order, key_live = jax.random.split(base_key, 4)
    busy_column = jax.random.randint(key_busy, (N_GY,), 0, N_GX)
    gx_column = jnp.arange(N_GX, dtype=jnp.int32)[:, None]
    needed = (busy_column[None, :] - gx_column) % N_GX
    pair_ids = jnp.arange(2 * REACH, dtype=jnp.int32)
    required = pair_ids[None, None, :] // 2 == needed[:, :, None]
    noise_bits = jax.random.randint(key_pick, (N_GX, N_GY, 2 * REACH), 0, 1 << 20)
    scores = noise_bits * (2 * REACH) + pair_ids + required.astype(jnp.int32) * (1 << 28)
    ranked = jnp.argsort(-scores, axis=-1)[..., :PAR_DEV]
    order_bits = jax.random.randint(key_order, (N_GX, N_GY, PAR_DEV), 0, 1 << 20) * PAR_DEV + jnp.arange(PAR_DEV, dtype=jnp.int32)
    shuffle = jnp.argsort(order_bits, axis=-1)
    chosen = jnp.take_along_axis(ranked, shuffle, axis=-1).astype(jnp.int32)
    is_required = chosen // 2 == needed[:, :, None]
    is_live = is_required | (jax.random.randint(key_live, (N_GX, N_GY, PAR_DEV), 0, 4) > 0)
    refine = jnp.where(is_live, chosen, -1)
    matches = (chosen[..., :, None] == pair_ids) & is_live[..., None]
    parent_table = jnp.where(jnp.any(matches, axis=2), jnp.sum(matches.astype(jnp.int32) * jnp.arange(PAR_DEV, dtype=jnp.int32)[:, None], axis=2), -1)
    sources = (gx_column - pair_ids[None, :] // 2) % N_GX
    parents = parent_table[sources[:, None, :], jnp.arange(N_GY, dtype=jnp.int32)[None, :, None], pair_ids[None, None, :]]
    return (refine.reshape(-1).astype(jnp.int32), parents.reshape(-1).astype(jnp.int32))


def draw_refine_to(key, part):
    return build_maps(key)[0]


def draw_parent_of(key, part):
    return build_maps(key)[1]


def block_scale(own_key, extent, shards, smallest, top_value):
    def one(dim, shards_of):
        draws = jax.random.uniform(jax.random.fold_in(jax.random.fold_in(own_key, 6), dim), (shards_of,), jnp.float32, smallest / len(shards), top_value / len(shards))
        return jnp.repeat(jnp.exp(draws), extent[dim] // shards_of).reshape((-1,) + (1,) * (len(extent) - dim - 1))

    gain = one(*shards[0])
    for cut in shards[1:]:
        gain = gain * one(*cut)
    return gain


def normal_values(rng, shape, deviation, limit, shards=(), kind=jnp.bfloat16):
    values = jax.random.normal(rng, shape, jnp.float32) * deviation
    if len(shards) > 0:
        values = block_scale(rng, shape, shards, -0.22, 0.18) * values
    return jnp.clip(values, min=-limit, max=limit).astype(kind)


def setup_inputs(seed: int = 0) -> dict:
    key_list = jax.random.split(jax.random.key(seed), 9)
    coarse_state = normal_values(key_list[0], (F, NX, NY * NZ), 1.0, 6.0, ((1, 16), (2, 2)), jnp.float32)
    coarse_rate = jnp.clip(jnp.exp(math.log(2.0) - 1.3862944 * jax.random.uniform(key_list[1], (NX, NY * NZ), jnp.float32) ** block_scale(key_list[1], (NX, NY * NZ), ((0, 16), (1, 2)), -0.2, 0.2)), 0.5, 2.0)
    fine_state = normal_values(key_list[2], (SLOTS, F, CX, CY * FZ), 1.0, 6.0, ((0, 32),), jnp.float32)
    fine_rate = jnp.clip(jnp.exp(math.log(2.0) - 1.3862944 * jax.random.uniform(key_list[3], (SLOTS, CX, CY * FZ), jnp.float32) ** block_scale(key_list[3], (SLOTS, CX, CY * FZ), ((0, 32),), -0.2, 0.2)), 0.5, 2.0)
    refine_to = draw_refine_to(jax.random.fold_in(key_list[8], 71), 0)
    parent_of = draw_parent_of(jax.random.fold_in(key_list[8], 71), 0)
    kappa = jnp.clip(jnp.exp(jax.random.uniform(key_list[6], (F,), jnp.float32, math.log(0.01), math.log(0.05))), 0.01, 0.05)
    reaction = normal_values(key_list[7], (F, F), F ** -0.5, 1.25, (), jnp.float32)
    return dict(coarse_state=coarse_state, coarse_rate=coarse_rate, fine_state=fine_state, fine_rate=fine_rate, refine_to=refine_to, parent_of=parent_of, kappa=kappa, reaction=reaction)


highest_mode = lax.Precision.HIGHEST


def transport(padded, diffusion, courant):
    center = padded[..., 1:-1, 1:-1, :]
    lateral = padded[..., 2:, 1:-1, :] + padded[..., :-2, 1:-1, :] + padded[..., 1:-1, 2:, :] + padded[..., 1:-1, :-2, :]
    lower_z = jnp.roll(center, 1, axis=-1)
    upper_z = jnp.roll(center, -1, axis=-1)
    laplacian = lateral + lower_z + upper_z - 6.0 * center
    return center + diffusion * laplacian - courant * (center - lower_z)


def react(fields, rate_field, time_step, reaction):
    for substep in range(SUBSTEPS):
        fields = fields + (time_step / SUBSTEPS) * rate_field * jnp.einsum("fg,...gxyz->...fxyz", reaction, fields, precision=highest_mode)
    return fields


def fine_steps(patches, patch_rates, cycle_old, cycle_mid, kappa, reaction):
    for cycle_now in (cycle_old, cycle_mid):
        upsampled = jnp.repeat(jnp.repeat(jnp.repeat(cycle_now, 2, axis=-3), 2, axis=-2), 2, axis=-1)
        padded = upsampled[..., 1:-1, 1:-1, :].at[..., 1:-1, 1:-1, :].set(patches)
        patches = react(transport(padded, 2.0 * kappa[:, None, None, None], 0.25), patch_rates[:, None], 0.5, reaction)
    return patches


def coarse_means(patches):
    count, fields, size_x, size_y, size_z = patches.shape
    return patches.reshape(count, fields, size_x // 2, 2, size_y // 2, 2, size_z // 2, 2).mean(axis=(3, 5, 7))


def reference(coarse_state, coarse_rate, fine_state, fine_rate, refine_to, parent_of, kappa, reaction):
    half_x = CX // 2
    half_y = CY // 2
    fine_z = 2 * NZ
    coarse_grid = coarse_state.reshape(F, NX, NY, NZ)
    rate_grid = coarse_rate.reshape(NX, NY, NZ)
    diffusion = kappa[:, None, None, None]
    wrap_pad = ((0, 0), (1, 1), (1, 1), (0, 0))
    padded_old = jnp.pad(coarse_grid, wrap_pad, mode="wrap")
    coarse_new = react(transport(padded_old, diffusion, 0.25), rate_grid, 1.0, reaction)
    padded_new = jnp.pad(coarse_new, wrap_pad, mode="wrap")

    def cut_cycle(field, start_x, start_y):
        return lax.dynamic_slice(field, (jnp.int32(0), start_x, start_y, jnp.int32(0)), (F, half_x + 2, half_y + 2, NZ))

    def one_device(inputs):
        patches, patch_rates, parents, device = inputs
        gx_index = device // N_GY
        gy_index = device % N_GY
        slot_ids = jnp.arange(SLOT_DEV, dtype=jnp.int32)
        sources = (gx_index - slot_ids // 2) % N_GX
        chosen = jnp.maximum(parents, 0)
        starts_x = (sources * CX + half_x * (chosen // 2)).astype(jnp.int32)
        starts_y = (gy_index * CY + half_y * (chosen % 2)).astype(jnp.int32)
        cycle_old = jax.vmap(cut_cycle, in_axes=(None, 0, 0))(padded_old, starts_x, starts_y)
        cycle_new = jax.vmap(cut_cycle, in_axes=(None, 0, 0))(padded_new, starts_x, starts_y)
        advanced = fine_steps(patches, patch_rates, cycle_old, 0.5 * (cycle_old + cycle_new), kappa, reaction)
        is_live = parents >= 0
        finished = jnp.where(is_live[:, None, None, None, None], advanced, 0.0)
        return finished, coarse_means(finished)

    device_ids = jnp.arange(DEVICES, dtype=jnp.int32)
    fine_out, averages = lax.map(one_device, (fine_state.reshape(DEVICES, SLOT_DEV, F, CX, CY, fine_z), fine_rate.reshape(DEVICES, SLOT_DEV, CX, CY, fine_z), parent_of.reshape(DEVICES, SLOT_DEV), device_ids))
    fine_out = fine_out.reshape(fine_state.shape)
    averages = averages.reshape(SLOTS, F, half_x, half_y, NZ)
    parent_ids = jnp.arange(PARENTS, dtype=jnp.int32)
    home_device = parent_ids // PAR_DEV
    gx_home = home_device // N_GY
    gy_home = home_device % N_GY
    chosen = jnp.maximum(refine_to, 0)
    owner_device = ((gx_home + chosen // 2) % N_GX) * N_GY + gy_home
    averaged = averages[(owner_device * SLOT_DEV + chosen).astype(jnp.int32)]
    coarse_parts = coarse_new.reshape(F, N_GX, 2, half_x, N_GY, 2, half_y, NZ).transpose(1, 4, 2, 5, 0, 3, 6, 7).reshape(PARENTS, F, half_x, half_y, NZ)
    merged = jnp.where((refine_to >= 0)[:, None, None, None, None], averaged, coarse_parts)
    coarse_out = merged.reshape(N_GX, N_GY, 2, 2, F, half_x, half_y, NZ).transpose(4, 0, 2, 5, 1, 3, 6, 7).reshape(coarse_state.shape)
    return coarse_out, fine_out
```

```python
import functools
import jax
import jax.numpy as jnp
from jax import lax
from jax.experimental import pallas as pl
from jax.experimental.pallas import tpu as pltpu
from jax.sharding import PartitionSpec as P

MESH = pl.DeviceIdType.MESH
F32 = jnp.float32
BF16 = jnp.bfloat16


def lanes(rows):
    return lax.broadcasted_iota(jnp.int32, (rows, 128), 1)


def pick(table, index):
    return jnp.take_along_axis(table, index, axis=1)


def powers(reaction, fields):
    row = lax.broadcasted_iota(jnp.int32, (fields, 3 * fields), 0)
    col = lax.broadcasted_iota(jnp.int32, (fields, 3 * fields), 1)
    power = (col % fields == row).astype(F32)
    result = []
    for _ in range(4):
        power = jnp.dot(
            reaction, power, precision=lax.Precision.HIGHEST, preferred_element_type=F32
        )
        result.append(power)
    return result, col < 2 * fields


def chem_weights(power_list, high_part, step):
    parts = []
    for count, (choose, power) in enumerate(zip((4.0, 6.0, 4.0, 1.0), power_list)):
        value = power * (choose * step ** (count + 1))
        high = value.astype(BF16).astype(F32)
        parts.append(jnp.where(high_part, high, value - high))
    return jnp.concatenate(parts, axis=0).astype(BF16)


def chemistry(weights, values, rates, fields):
    wide = jnp.concatenate(values, axis=1)
    high = wide.astype(BF16).astype(F32)
    low = wide - high
    stacked = jnp.concatenate([high, low, high], axis=0).astype(BF16)
    product = jnp.dot(weights, stacked, preferred_element_type=F32)
    out = []
    for n, (value, rate) in enumerate(zip(values, rates)):
        part = [
            product[q * fields : (q + 1) * fields, n * 128 : (n + 1) * 128] for q in range(4)
        ]
        rate = jnp.broadcast_to(rate, value.shape)
        out.append(value + rate * (part[0] + rate * (part[1] + rate * (part[2] + rate * part[3]))))
    return out


def kernel(
    n_gx, n_gy, fields, size_x, slots,
    refine_hbm, parent_hbm, coarse_hbm, crate_hbm, fine_hbm, frate_hbm, kappa_hbm, reaction_hbm,
    cout, fout,
    refine_ref, parent_ref, kappa_ref, reaction_ref, cin, crate, fin, frate,
    buf_a, buf_b, row_send, col_send, hx, hy, cnew, cols, ring_local, ring_send, ring_recv,
    means, mean_send, mean_recv, wf_ref, wc_ref, rate8, edge_rate,
    in_sem, send_sem, recv_sem,
):
    F = fields
    fine_cols = frate.shape[2]
    gx = lax.axis_index("gx")
    gy = lax.axis_index("gy")
    right = lax.rem(gx + 1, n_gx)
    left = lax.rem(gx + n_gx - 1, n_gx)
    above = lax.rem(gy + 1, n_gy)
    below = lax.rem(gy + n_gy - 1, n_gy)

    barrier = pltpu.get_barrier_semaphore()
    for target in ((left, gy), (right, gy), (gx, below), (gx, above)):
        pl.semaphore_signal(barrier, inc=1, device_id=target, device_id_type=MESH)

    loads = [
        pltpu.make_async_copy(coarse_hbm, cin, in_sem.at[0]),
        pltpu.make_async_copy(crate_hbm, crate, in_sem.at[1]),
        pltpu.make_async_copy(frate_hbm, frate, in_sem.at[2]),
    ]
    fine_loads = []
    for s in range(slots):
        for h in range(2):
            fine_loads.append(
                pltpu.make_async_copy(
                    fine_hbm.at[s, :, pl.ds(h * 128, 128)], fin.at[s, h], in_sem.at[3 + 2 * s + h]
                )
            )
    small = [
        pltpu.make_async_copy(reaction_hbm, reaction_ref, in_sem.at[11]),
        pltpu.make_async_copy(kappa_hbm, kappa_ref, in_sem.at[12]),
        pltpu.make_async_copy(refine_hbm, refine_ref, in_sem.at[13]),
        pltpu.make_async_copy(parent_hbm, parent_ref, in_sem.at[14]),
    ]
    for copy in loads[:1] + small + fine_loads + loads[1:]:
        copy.start()

    def send(n, src, dst, target):
        copy = pltpu.make_async_remote_copy(
            src_ref=src, dst_ref=dst, send_sem=send_sem.at[n], recv_sem=recv_sem.at[n],
            device_id=target, device_id_type=MESH,
        )
        copy.start()
        return copy

    lane = lanes(F)
    first_half = lane < 64

    def pack(rows_of, y):
        total = jnp.zeros((F, 128), F32)
        for x in range(size_x):
            shift = ((x - y) * 8) % 128
            row = rows_of(x)
            moved = pltpu.roll(row, shift, 1) if shift else row
            total = jnp.where(lane // 8 == x, moved, total)
        return total

    def halos(level):
        base = 4 * level
        return [
            send(base + 0, row_send.at[level, 1], hx.at[level, 0], (right, gy)),
            send(base + 1, row_send.at[level, 0], hx.at[level, 1], (left, gy)),
            send(base + 2, col_send.at[level, 1], hy.at[level, 0], (gx, above)),
            send(base + 3, col_send.at[level, 0], hy.at[level, 1], (gx, below)),
        ]

    loads[0].wait()
    old_rows = lambda x: cin[pl.ds(x, F, stride=size_x), :]
    row_send[0, 0] = old_rows(0)
    row_send[0, 1] = old_rows(size_x - 1)
    col_send[0, 0] = pack(old_rows, 0)
    col_send[0, 1] = pack(old_rows, size_x - 1)

    cols[0, 0] = pack(old_rows, size_x // 2 - 1)
    cols[0, 1] = pack(old_rows, size_x // 2)
    for copy in small:
        copy.wait()
    power_list, high_part = powers(reaction_ref[...], F)
    wf_ref[...] = chem_weights(power_list, high_part, 0.125)
    wc_ref[...] = chem_weights(power_list, high_part, 0.25)
    diag = lax.broadcasted_iota(jnp.int32, (F, F), 0) == lax.broadcasted_iota(jnp.int32, (F, F), 1)
    kappa_col = jnp.sum(
        jnp.where(diag, jnp.broadcast_to(kappa_ref[...], (F, F)), 0.0), axis=1, keepdims=True
    )
    kappa = jnp.broadcast_to(kappa_col, (F, 128))
    kappa2 = 2.0 * kappa

    for copy in fine_loads:
        copy.wait()
    for s in range(slots):
        for h in range(2):
            for x in range(size_x):
                buf_a[s, x + 1, :, pl.ds(h * 128, 128)] = fin[s, h, pl.ds(x, F, stride=size_x), :]
    loads[1].wait()
    loads[2].wait()
    for s in range(slots):
        for x in range(size_x):
            rate8[s, x] = jnp.broadcast_to(frate[s, pl.ds(x, 1), :], rate8.shape[2:])
    lane8 = lanes(8)
    for s in range(slots):
        for q in range(size_x // 4):
            total = jnp.zeros((8, 128), F32)
            for n in range(4):
                lo = rate8[s, 4 * q + n, :, pl.ds(0, 128)]
                hi = rate8[s, 4 * q + n, :, pl.ds(fine_cols - 128, 128)]
                lo = pltpu.roll(lo, 16 * n, 1) if n else lo
                shift = (16 * n - 48) % 128
                hi = pltpu.roll(hi, shift, 1) if shift else hi
                total = jnp.where(lane8 // 16 == n, lo, total)
                total = jnp.where(lane8 // 16 == 4 + n, hi, total)
            edge_rate[s, q] = total
    z16 = lane % 16
    row_index = (lane // 32) * 8 + z16 // 2
    col_index = jnp.where(lane < 64, 0, 64) + z16 // 2
    target = lane % 64
    mean_index = ((target // 8) % 4) * 32 + 2 * (target % 8)
    mean_low = target // 32 == 0

    def ring_of(level, s, side):
        return ring_local[level, s, side] if s < 2 else ring_recv[level, s - 2, side]

    def fine_step(s, step):
        src = buf_a if step == 0 else buf_b
        if step == 0:
            src[s, 0] = jnp.zeros((F, fine_cols), F32)
            src[s, size_x + 1] = jnp.zeros((F, fine_cols), F32)
        else:
            edge_x = 0.5 * (ring_of(0, s, 0) + ring_of(1, s, 0))
            edge_y = 0.5 * (ring_of(0, s, 1) + ring_of(1, s, 1))
            for h in range(2):
                src[s, 0, :, pl.ds(h * 128, 128)] = pick(edge_x, row_index + 32 * h)
                src[s, size_x + 1, :, pl.ds(h * 128, 128)] = pick(edge_x, row_index + 64 + 32 * h)
        weights = wf_ref[...]
        live = jnp.full((F, 128), parent_ref[s], jnp.int32) >= 0

        def pair(j, carry):
            ghost = pick(edge_y, col_index + 8 * j) if step else jnp.zeros((F, 128), F32)
            values, rates = [], []
            for n in range(2):
                x = 2 * j + n
                c = [src[s, x + 1, :, pl.ds(h * 128, 128)] for h in range(2)]
                up = [src[s, x, :, pl.ds(h * 128, 128)] for h in range(2)]
                dn = [src[s, x + 2, :, pl.ds(h * 128, 128)] for h in range(2)]
                ra = [pltpu.roll(v, 16, 1) for v in c]
                rb = [pltpu.roll(v, 112, 1) for v in c]
                yl = [jnp.where(lane < 16, ghost, ra[0]), jnp.where(lane < 16, ra[0], ra[1])]
                yh = [jnp.where(lane >= 112, rb[1], rb[0]), jnp.where(lane >= 112, ghost, rb[1])]
                for h in range(2):
                    v = c[h]
                    zl = jnp.where(z16 == 0, pltpu.roll(v, 113, 1), pltpu.roll(v, 1, 1))
                    zu = jnp.where(z16 == 15, pltpu.roll(v, 15, 1), pltpu.roll(v, 127, 1))
                    lap = (yl[h] + yh[h]) + (up[h] + dn[h]) + (zl + zu) - 6.0 * v
                    values.append(v + kappa2 * lap - 0.25 * (v - zl))
                    rate = rate8[s, x, :, pl.ds(h * 128, 128)]
                    rates.append(jnp.concatenate([rate] * (F // 8), axis=0))
            new = chemistry(weights, values, rates, F)
            if step == 0:
                for n in range(2):
                    for h in range(2):
                        buf_b[s, 2 * j + n + 1, :, pl.ds(h * 128, 128)] = new[2 * n + h]
            else:
                new = [jnp.where(live, v, 0.0) for v in new]
                for n in range(2):
                    for h in range(2):
                        fout[s, h, pl.ds(2 * j + n, F, stride=size_x), :] = new[2 * n + h]
                picked = []
                for h in range(2):
                    total = new[h] + new[2 + h]
                    total = total + pltpu.roll(total, 127, 1)
                    total = total + pltpu.roll(total, 112, 1)
                    picked.append(pick(total, mean_index))
                means[s, j] = 0.125 * jnp.where(mean_low, picked[0], picked[1])
            return carry

        lax.fori_loop(0, size_x // 2, pair, 0, unroll=4)

    edge_index = (lane // 64) * 64 + ((lane % 64) // 32) * 8 + z16 // 2

    def wide_rate(rate):
        return jnp.concatenate([rate] * (F // 8), axis=0)

    def correct(s):
        edge_x, edge_y = ring_of(0, s, 0), ring_of(0, s, 1)
        values, rates = [], []
        for side, x in ((0, 0), (1, size_x - 1)):
            for h in range(2):
                values.append(kappa2 * pick(edge_x, row_index + 64 * side + 32 * h))
                rates.append(wide_rate(rate8[s, x, :, pl.ds(h * 128, 128)]))
        for q in range(size_x // 4):
            values.append(kappa2 * pick(edge_y, edge_index + 16 * q))
            rates.append(wide_rate(edge_rate[s, q]))
        share = chemistry(wf_ref[...], values, rates, F)
        for x in range(size_x):
            q, n = x // 4, x % 4
            both = share[4 + q]
            lo = pltpu.roll(both, (-16 * n) % 128, 1) if n else both
            shift = (48 - 16 * n) % 128
            hi = pltpu.roll(both, shift, 1) if shift else both
            added = [jnp.where(lane < 16, lo, 0.0), jnp.where(lane >= 112, hi, 0.0)]
            for h in range(2):
                if x == 0:
                    added[h] = added[h] + share[h]
                if x == size_x - 1:
                    added[h] = added[h] + share[2 + h]
                here = (s, x + 1, slice(None), pl.ds(h * 128, 128))
                buf_b[here] = buf_b[here] + added[h]

    for s in ():
        fine_step(s, 0)
    pl.semaphore_wait(barrier, 4)
    old_halos = halos(0)
    for s in (0, 1):
        fine_step(s, 0)
    for copy in old_halos:
        copy.wait_recv()

    z8 = lane % 8
    for group in range(size_x // 4):
        values, rates = [], []
        for x in range(4 * group, 4 * group + 4):
            c = old_rows(x)
            up = old_rows(x - 1) if x > 0 else hx[0, 0]
            dn = old_rows(x + 1) if x < size_x - 1 else hx[0, 1]
            ghost_lo = pltpu.roll(hy[0, 0], (-x * 8) % 128, 1) if x else hy[0, 0]
            shift = (120 - x * 8) % 128
            ghost_hi = pltpu.roll(hy[0, 1], shift, 1) if shift else hy[0, 1]
            yl = jnp.where(lane < 8, ghost_lo, pltpu.roll(c, 8, 1))
            yh = jnp.where(lane >= 120, ghost_hi, pltpu.roll(c, 120, 1))
            zl = jnp.where(z8 == 0, pltpu.roll(c, 121, 1), pltpu.roll(c, 1, 1))
            zu = jnp.where(z8 == 7, pltpu.roll(c, 7, 1), pltpu.roll(c, 127, 1))
            lap = (yl + yh) + (up + dn) + (zl + zu) - 6.0 * c
            values.append(c + kappa * lap - 0.25 * (c - zl))
            rates.append(crate[pl.ds(x, 1), :])
        for n, new in enumerate(chemistry(wc_ref[...], values, rates, F)):
            cnew[4 * group + n] = new
    new_rows = lambda x: cnew[x]
    row_send[1, 0] = new_rows(0)
    row_send[1, 1] = new_rows(size_x - 1)
    col_send[1, 0] = pack(new_rows, 0)
    col_send[1, 1] = pack(new_rows, size_x - 1)
    new_halos = halos(1)

    parents = [jnp.full((F, 128), refine_ref[p], jnp.int32) for p in range(4)]

    def rings(level, rows_of):
        mid = size_x // 2
        row_at = (hx[level, 0], rows_of(mid - 1), rows_of(mid), hx[level, 1])
        col_at = (hy[level, 0], cols[level, 0], cols[level, 1], hy[level, 1])

        def joined(lo, hi, half):
            if half == 0:
                return jnp.where(first_half, lo, pltpu.roll(hi, 64, 1))
            return jnp.where(first_half, pltpu.roll(lo, 64, 1), hi)

        all_rings = []
        for p in range(4):
            a, b = p // 2, p % 2
            all_rings.append(
                (joined(row_at[a], row_at[a + 2], b), joined(col_at[b], col_at[b + 2], a))
            )
        for k in range(4):
            for side in range(2):
                value = jnp.zeros((F, 128), F32)
                for p in range(4):
                    value = jnp.where(parents[p] == k, all_rings[p][side], value)
                if k < 2:
                    ring_local[level, k, side] = value
                else:
                    ring_send[level, k - 2, side] = value
        return send(8 + level, ring_send.at[level], ring_recv.at[level], (right, gy))

    ring_old = rings(0, old_rows)
    cols[1, 0] = pack(new_rows, size_x // 2 - 1)
    cols[1, 1] = pack(new_rows, size_x // 2)

    half = size_x // 4

    def send_means(s):
        for j in range(half):
            mean_send[s - 2, j] = jnp.where(first_half, means[s, j], means[s, j + half])
        return send(8 + s, mean_send.at[s - 2], mean_recv.at[s - 2], (left, gy))

    for s in (2, 3):
        fine_step(s, 0)
    correct(0)
    correct(1)
    for copy in new_halos:
        copy.wait_recv()
    ring_new = rings(1, new_rows)
    fine_step(0, 1)
    ring_old.wait_recv()
    correct(2)
    correct(3)
    ring_new.wait_recv()
    fine_step(2, 1)
    sent_2 = send_means(2)
    fine_step(3, 1)
    sent_3 = send_means(3)
    fine_step(1, 1)
    sent_2.wait_recv()
    sent_3.wait_recv()

    for x in range(size_x):
        a, X = x // (size_x // 2), x % (size_x // 2)
        full = [means[0, X], means[1, X]]
        for k in range(2):
            packed = mean_recv[k, X % half]
            turned = pltpu.roll(packed, 64, 1)
            low, high = (packed, turned) if X < half else (turned, packed)
            full.append(jnp.where(first_half, low, high))
        owner = jnp.where(first_half, parents[2 * a], parents[2 * a + 1])
        value = new_rows(x)
        for k in range(4):
            value = jnp.where(owner == k, full[k], value)
        cout[pl.ds(x, F, stride=size_x), :] = value
    for copy in old_halos + new_halos + [ring_old, ring_new, sent_2, sent_3]:
        copy.wait_send()


def store_kernel(cout, fout, coarse_out_hbm, fine_out_hbm, sem):
    copies = [pltpu.make_async_copy(cout, coarse_out_hbm, sem.at[0])]
    slots = fout.shape[0]
    for s in range(slots):
        for h in range(2):
            copies.append(
                pltpu.make_async_copy(
                    fout.at[s, h], fine_out_hbm.at[s, :, pl.ds(h * 128, 128)],
                    sem.at[1 + 2 * s + h],
                )
            )
    for copy in copies:
        copy.start()
    for copy in copies:
        copy.wait()


def body(coarse_state, coarse_rate, fine_state, fine_rate, refine_to, parent_of, kappa, reaction):
    fields, size_x, merged = coarse_state.shape
    slots = fine_state.shape[0]
    fine_merged = fine_state.shape[3]
    flat = fields * size_x
    any_spec = pl.BlockSpec(memory_space=pl.ANY)
    vmem = pl.BlockSpec(memory_space=pltpu.VMEM)
    V = pltpu.VMEM
    tile = (fields, 128)
    cout, fout = pl.pallas_call(
        functools.partial(
            kernel, lax.axis_size("gx"), lax.axis_size("gy"), fields, size_x, slots
        ),
        out_shape=(V((flat, 128), F32), V((slots, 2, flat, 128), F32)),
        in_specs=[any_spec] * 8,
        out_specs=(vmem, vmem),
        scratch_shapes=[
            pltpu.SMEM((slots,), jnp.int32),
            pltpu.SMEM((slots,), jnp.int32),
            V((1, fields), F32),
            V((fields, fields), F32),
            V((flat, 128), F32),
            V((size_x, 128), F32),
            V((slots, 2, flat, 128), F32),
            V((slots, size_x, fine_merged), F32),
            V((slots, size_x + 2, fields, fine_merged), F32),
            V((slots, size_x + 2, fields, fine_merged), F32),
            V((2, 2) + tile, F32),
            V((2, 2) + tile, F32),
            V((2, 2) + tile, F32),
            V((2, 2) + tile, F32),
            V((size_x,) + tile, F32),
            V((2, 2) + tile, F32),
            V((2, 2, 2) + tile, F32),
            V((2, 2, 2) + tile, F32),
            V((2, 2, 2) + tile, F32),
            V((slots, size_x // 2) + tile, F32),
            V((2, size_x // 4) + tile, F32),
            V((2, size_x // 4) + tile, F32),
            V((4 * fields, 3 * fields), BF16),
            V((4 * fields, 3 * fields), BF16),
            V((slots, size_x, 8, fine_merged), F32),
            V((slots, size_x // 4, 8, 128), F32),
            pltpu.SemaphoreType.DMA((15,)),
            pltpu.SemaphoreType.DMA((12,)),
            pltpu.SemaphoreType.DMA((12,)),
        ],
        compiler_params=pltpu.CompilerParams(
            collective_id=0, has_side_effects=True, vmem_limit_bytes=24 * 2**20
        ),
    )(
        *[
            pltpu.with_memory_space_constraint(array, pltpu.HBM)
            for array in (
                refine_to, parent_of, coarse_state.reshape(flat, merged), coarse_rate,
                fine_state.reshape(slots, flat, fine_merged), fine_rate,
                kappa.reshape(1, fields), reaction,
            )
        ]
    )
    coarse_out, fine_out = pl.pallas_call(
        store_kernel,
        out_shape=(
            jax.ShapeDtypeStruct((flat, merged), F32),
            jax.ShapeDtypeStruct((slots, flat, fine_merged), F32),
        ),
        in_specs=[vmem, vmem],
        out_specs=(any_spec, any_spec),
        scratch_shapes=[pltpu.SemaphoreType.DMA((1 + 2 * slots,))],
        compiler_params=pltpu.CompilerParams(vmem_limit_bytes=8 * 2**20),
    )(cout, fout)
    return coarse_out.reshape(coarse_state.shape), fine_out.reshape(fine_state.shape)


def solution(mesh):
    in_specs = (
        P(None, "gx", "gy"),
        P("gx", "gy"),
        P(("gx", "gy"), None, None, None),
        P(("gx", "gy"), None, None),
        P(("gx", "gy")),
        P(("gx", "gy")),
        P(),
        P(),
    )
    out_specs = (P(None, "gx", "gy"), P(("gx", "gy"), None, None, None))
    return jax.shard_map(body, mesh=mesh, in_specs=in_specs, out_specs=out_specs, check_vma=False)
```

```python
import functools
import jax
import jax.numpy as jnp
from jax import lax
from jax.experimental import pallas as pl
from jax.experimental.pallas import tpu as pltpu
from jax.sharding import PartitionSpec as P

MESH = pl.DeviceIdType.MESH
F32 = jnp.float32
BF16 = jnp.bfloat16


def lanes(rows):
    return lax.broadcasted_iota(jnp.int32, (rows, 128), 1)


def pick(table, index):
    return jnp.take_along_axis(table, index, axis=1)


def powers(reaction, fields):
    row = lax.broadcasted_iota(jnp.int32, (fields, 3 * fields), 0)
    col = lax.broadcasted_iota(jnp.int32, (fields, 3 * fields), 1)
    power = (col % fields == row).astype(F32)
    result = []
    for _ in range(4):
        power = jnp.dot(
            reaction, power, precision=lax.Precision.HIGHEST, preferred_element_type=F32
        )
        result.append(power)
    return result, col < 2 * fields


def chem_weights(power_list, high_part, step):
    parts = []
    for count, (choose, power) in enumerate(zip((4.0, 6.0, 4.0, 1.0), power_list)):
        value = power * (choose * step ** (count + 1))
        high = value.astype(BF16).astype(F32)
        parts.append(jnp.where(high_part, high, value - high))
    return jnp.concatenate(parts, axis=0).astype(BF16)


def chemistry(weights, values, rates, fields):
    wide = jnp.concatenate(values, axis=1)
    high = wide.astype(BF16).astype(F32)
    low = wide - high
    stacked = jnp.concatenate([high, low, high], axis=0).astype(BF16)
    product = jnp.dot(weights, stacked, preferred_element_type=F32)
    out = []
    for n, (value, rate) in enumerate(zip(values, rates)):
        part = [
            product[q * fields : (q + 1) * fields, n * 128 : (n + 1) * 128] for q in range(4)
        ]
        rate = jnp.broadcast_to(rate, value.shape)
        out.append(value + rate * (part[0] + rate * (part[1] + rate * (part[2] + rate * part[3]))))
    return out


def shift_matrix(group):
    row = lax.broadcasted_iota(jnp.int32, (256, 128), 0) % 128
    col = lax.broadcasted_iota(jnp.int32, (256, 128), 1)
    same = row // group == col // group
    lower = same & ((col - row + group) % group == 1)
    upper = same & ((row - col + group) % group == 1)
    side = (row - col == group) | (col - row == group)
    around = jnp.where(lower | upper | side, 1.0, 0.0)
    return jnp.concatenate([around, jnp.where(lower, 0.25, 0.0)], axis=1).astype(BF16)


def shifted_sums(matrix, rows):
    high = rows.astype(BF16)
    low = (rows - high.astype(F32)).astype(BF16)
    return jnp.dot(
        jnp.concatenate([high, low], axis=1), matrix, preferred_element_type=F32
    )


def turn(value, shift):
    shift = shift % 128
    return pltpu.roll(value, shift, 1) if shift else value


def kernel(
    n_gx, n_gy, fields, size_x, slots,
    refine_hbm, parent_hbm, coarse_hbm, crate_hbm, fine_hbm, frate_hbm, kappa_hbm, reaction_hbm,
    cout, fout,
    refine_ref, parent_ref, kappa_ref, reaction_ref, cin, crate, fin, frate, buf_b,
    row_send, col_send, corner_send, rx, ry, rd, cnew, cols, rate_cols,
    ring, ring_send, ring_recv, means, mean_send, mean_recv,
    cols_new, wf_ref, wc_ref, rate8, edge_rate, shift_f, shift_c,
    in_sem, send_sem, recv_sem,
):
    F = fields
    fine_cols = frate.shape[2]
    last = size_x - 1
    mid = size_x // 2
    gx = lax.axis_index("gx")
    gy = lax.axis_index("gy")
    right = lax.rem(gx + 1, n_gx)
    left = lax.rem(gx + n_gx - 1, n_gx)
    above = lax.rem(gy + 1, n_gy)
    below = lax.rem(gy + n_gy - 1, n_gy)

    barrier = pltpu.get_barrier_semaphore()
    for target in (
        (right, gy), (left, gy), (gx, above), (gx, below),
        (right, above), (right, below), (left, above), (left, below),
    ):
        pl.semaphore_signal(barrier, inc=1, device_id=target, device_id_type=MESH)

    load_coarse = pltpu.make_async_copy(coarse_hbm, cin, in_sem.at[0])
    load_crate = pltpu.make_async_copy(crate_hbm, crate, in_sem.at[1])
    load_frate = pltpu.make_async_copy(frate_hbm, frate, in_sem.at[2])
    fine_loads = [
        [
            pltpu.make_async_copy(
                fine_hbm.at[s, :, pl.ds(h * 128, 128)], fin.at[s, h], in_sem.at[3 + 2 * s + h]
            )
            for h in range(2)
        ]
        for s in range(slots)
    ]
    small = [
        pltpu.make_async_copy(reaction_hbm, reaction_ref, in_sem.at[11]),
        pltpu.make_async_copy(kappa_hbm, kappa_ref, in_sem.at[12]),
        pltpu.make_async_copy(refine_hbm, refine_ref, in_sem.at[13]),
        pltpu.make_async_copy(parent_hbm, parent_ref, in_sem.at[14]),
    ]
    order = (2, 3, 0, 1)
    for copy in [load_coarse, load_crate] + small + [load_frate]:
        copy.start()
    for s in order:
        for copy in fine_loads[s]:
            copy.start()

    def send(n, src, dst, target):
        copy = pltpu.make_async_remote_copy(
            src_ref=src, dst_ref=dst, send_sem=send_sem.at[n], recv_sem=recv_sem.at[n],
            device_id=target, device_id_type=MESH,
        )
        copy.start()
        return copy

    lane = lanes(F)
    lane8 = lanes(8)
    first_half = lane < 64

    shift_f[...] = shift_matrix(16)
    shift_c[...] = shift_matrix(8)

    def pack(rows_of, y, at):
        total = None
        for x in range(size_x):
            moved = turn(rows_of(x), (x - y) * 8)
            total = moved if total is None else jnp.where(at // 8 == x, moved, total)
        return total

    near, far, rate_rows = pl.ds(0, F), pl.ds(F, F), pl.ds(2 * F, 8)
    old_row = lambda x: cin[pl.ds(x, F, stride=size_x), :]
    crate_row = lambda x: jnp.broadcast_to(crate[pl.ds(x, 1), :], (8, 128))

    load_coarse.wait()
    load_crate.wait()
    for side, (x0, x1) in enumerate(((0, 1), (last, last - 1))):
        row, rate = old_row(x0), crate_row(x0)
        row_send[side, near] = row
        row_send[side, far] = old_row(x1)
        row_send[side, rate_rows] = rate
        pieces = [row[8 * j : 8 * j + 8] for j in range(F // 8)] + [rate]
        corner = pieces[0]
        for j, piece in enumerate(pieces):
            if j:
                corner = jnp.where(lane8 // 8 == j, turn(piece, 8 * j), corner)
            corner = jnp.where(lane8 // 8 == 8 + j, turn(piece, 8 * j - 56), corner)
        corner_send[side] = corner
    for side, (y0, y1) in enumerate(((0, 1), (last, last - 1))):
        col_send[side, near] = pack(old_row, y0, lane)
        col_send[side, far] = pack(old_row, y1, lane)
        col_send[side, rate_rows] = pack(crate_row, y0, lane8)

    for copy in small:
        copy.wait()
    power_list, high_part = powers(reaction_ref[...], F)
    wf_ref[...] = chem_weights(power_list, high_part, 0.125)
    wc_ref[...] = chem_weights(power_list, high_part, 0.25)
    diag = lax.broadcasted_iota(jnp.int32, (F, F), 0) == lax.broadcasted_iota(jnp.int32, (F, F), 1)
    kappa_col = jnp.sum(
        jnp.where(diag, jnp.broadcast_to(kappa_ref[...], (F, F)), 0.0), axis=1, keepdims=True
    )
    kappa = jnp.broadcast_to(kappa_col, (F, 128))
    kappa2 = 2.0 * kappa
    keep_fine = 0.75 - 6.0 * kappa2
    keep_coarse = 0.75 - 6.0 * kappa

    pl.semaphore_wait(barrier, 8)
    to_right = [
        send(0, row_send.at[1], rx.at[0], (right, gy)),
        send(4, corner_send.at[1], rd.at[0], (right, above)),
        send(5, corner_send.at[1], rd.at[1], (right, below)),
    ]
    to_side = [
        send(2, col_send.at[1], ry.at[0], (gx, above)),
        send(3, col_send.at[0], ry.at[1], (gx, below)),
    ]
    to_left = [
        send(1, row_send.at[0], rx.at[1], (left, gy)),
        send(6, corner_send.at[0], rd.at[2], (left, above)),
        send(7, corner_send.at[0], rd.at[3], (left, below)),
    ]
    for n in range(4):
        cols[n] = pack(old_row, mid - 2 + n, lane)
    for n in range(2):
        rate_cols[n] = pack(crate_row, mid - 1 + n, lane8)

    def wide(rate):
        return jnp.concatenate([rate] * (F // 8), axis=0)

    def from_corner(m, src, dst):
        tile = rd[m]
        return jnp.concatenate([turn(tile, dst - src - 8 * j) for j in range(F // 8)], axis=0)

    def coarse_tiles(tiles):
        centers = jnp.concatenate([tile[0] for tile in tiles], axis=0)
        shifted = shifted_sums(shift_c[...], centers)
        values = []
        for n, (center, lo, hi, ghost_lo, ghost_hi, _) in enumerate(tiles):
            part = shifted[F * n : F * n + F]
            edge = 0.0 if ghost_hi is None else jnp.where(lane >= 120, ghost_hi, 0.0)
            edge = jnp.where(lane < 8, ghost_lo, edge)
            lateral = (lo + hi) + (part[:, :128] + edge)
            values.append(keep_coarse * center + kappa * lateral + part[:, 128:])
        return values

    def react(values, rates):
        out = []
        for at in range(0, len(values), 4):
            out += chemistry(wc_ref[...], values[at : at + 4], rates[at : at + 4], F)
        return out

    def row_tile(x):
        if x == -1:
            return (
                rx[0, near], rx[0, far], old_row(0),
                from_corner(0, 64, 0), from_corner(1, 0, 120), wide(rx[0, rate_rows]),
            )
        if x == size_x:
            return (
                rx[1, near], old_row(last), rx[1, far],
                from_corner(2, 64, 0), from_corner(3, 0, 120), wide(rx[1, rate_rows]),
            )
        return (
            old_row(x),
            old_row(x - 1) if x else rx[0, near],
            old_row(x + 1) if x < last else rx[1, near],
            turn(ry[0, near], -8 * x), turn(ry[1, near], 120 - 8 * x),
            crate[pl.ds(x, 1), :],
        )

    def joined(lo, hi, half):
        if half == 0:
            return jnp.where(first_half, lo, turn(hi, 64))
        return jnp.where(first_half, turn(lo, 64), hi)

    parents = [jnp.full((F, 128), refine_ref[p], jnp.int32) for p in range(4)]

    def ring_tiles(row_at, col_at):
        return [
            (
                joined(row_at[p // 2], row_at[p // 2 + 2], p % 2),
                joined(col_at[p % 2], col_at[p % 2 + 2], p // 2),
            )
            for p in range(4)
        ]

    def chosen(tiles, k, side):
        value = jnp.zeros((F, 128), F32)
        for p in range(4):
            value = jnp.where(parents[p] == k, tiles[p][side], value)
        return value

    def send_ring(level, row_at, col_at):
        tiles = ring_tiles(row_at, col_at)
        for k in range(2):
            for side in range(2):
                ring_send[level, k, side] = chosen(tiles, k + 2, side)
        return send(8 + level, ring_send.at[level], ring_recv.at[level], (right, gy))

    corner_lanes = (lane // 8 == 7) | (lane // 8 == 15)

    def end_share(share):
        return (
            jnp.where(corner_lanes, turn(share, 56), 0.0), jnp.where(corner_lanes, share, 0.0)
        )

    for copy in to_right + to_side:
        copy.wait_recv()
    old_cols = [ry[0, near], cols[1], cols[2], ry[1, near]]
    ring_old = send_ring(
        0, [rx[0, near], old_row(mid - 1), old_row(mid), old_row(mid)], old_cols
    )
    tiles = [
        row_tile(-1), row_tile(mid - 1), row_tile(mid), row_tile(0),
        (ry[0, near], ry[0, far], col_send[0, near], from_corner(0, 64, 0), None,
         wide(ry[0, rate_rows])),
        (cols[1], cols[0], cols[2], turn(rx[0, near], -8 * (mid - 1)), None, wide(rate_cols[0])),
        (cols[2], cols[1], cols[3], turn(rx[0, near], -8 * mid), None, wide(rate_cols[1])),
        (ry[1, near], col_send[1, near], ry[1, far], from_corner(1, 0, 0), None,
         wide(ry[1, rate_rows])),
    ]
    values = coarse_tiles(tiles)
    end = jnp.where(lane >= 120, turn(ry[1, near], 120), old_row(0))
    values.append(kappa * jnp.where(lane < 8, ry[0, near], end))
    end_rate = jnp.where(lane8 >= 120, turn(rd[1], 96), rx[0, rate_rows])
    end_rate = jnp.where(lane8 < 8, turn(rd[0], 40), end_rate)
    result = react(values, [tile[5] for tile in tiles] + [wide(end_rate)])
    new_before, new_cols = result[0], result[4:8]
    cnew[mid - 1], cnew[mid], cnew[0] = result[1:4]
    ring_new = send_ring(1, [new_before, result[1], result[2], result[2]], new_cols)
    far_share = result[8]
    for n, value in enumerate([new_before] + new_cols):
        cols_new[n] = value
    cols_new[5] = far_share

    z16 = lane % 16
    row_index = (lane // 32) * 8 + z16 // 2
    col_index = jnp.where(lane < 64, 0, 64) + z16 // 2
    target = lane % 64
    mean_index = ((target // 8) % 4) * 32 + 2 * (target % 8)
    mean_low = target // 32 == 0
    edge_lane = (lane < 16) | (lane >= 112)

    load_frate.wait()

    def spread_rate(s):
        for x in range(size_x):
            rate8[s, x] = jnp.broadcast_to(frate[s, pl.ds(x, 1), :], rate8.shape[2:])

    def fine_step(s, step, edges, done=None):
        def row_of(x, h):
            if 0 <= x < size_x:
                if step == 0:
                    return fin[s, h, pl.ds(x, F, stride=size_x), :]
                return buf_b[s, x, :, pl.ds(h * 128, 128)]
            if edges is None:
                return jnp.zeros((F, 128), F32)
            return pick(edges[0], row_index + 32 * h + (64 if x > 0 else 0))

        weights = wf_ref[...]
        live = jnp.full((F, 128), parent_ref[s], jnp.int32) >= 0
        size = size_x // 2
        for i in range(2):
            rows = [[row_of(x, h) for h in range(2)] for x in range(size * i - 1, size * i + size + 1)]
            shifted = shifted_sums(
                shift_f[...], jnp.concatenate([v for row in rows[1:-1] for v in row], axis=0)
            )
            for m in range(size // 2):
                j = size // 2 * i + m
                if edges is None:
                    ghost = 0.0
                else:
                    ghost = jnp.where(edge_lane, pick(edges[1], col_index + 8 * j), 0.0)
                values, rates = [], []
                for n in range(2):
                    r = 2 * m + n + 1
                    v0, v1 = rows[r]
                    cross = [
                        jnp.where(lane >= 112, turn(v1, 112), ghost),
                        jnp.where(lane < 16, turn(v0, 16), ghost),
                    ]
                    for h in range(2):
                        at = F * (2 * (r - 1) + h)
                        part = shifted[at : at + F]
                        lateral = (part[:, :128] + cross[h]) + (rows[r - 1][h] + rows[r + 1][h])
                        values.append(keep_fine * rows[r][h] + kappa2 * lateral + part[:, 128:])
                        rates.append(wide(rate8[s, 2 * j + n, :, pl.ds(h * 128, 128)]))
                new = chemistry(weights, values, rates, F)
                if step == 0:
                    for n in range(2):
                        for h in range(2):
                            buf_b[s, 2 * j + n, :, pl.ds(h * 128, 128)] = new[2 * n + h]
                else:
                    new = [jnp.where(live, v, 0.0) for v in new]
                    for n in range(2):
                        for h in range(2):
                            fout[s, h, pl.ds(2 * j + n, F, stride=size_x), :] = new[2 * n + h]
                    picked = []
                    for h in range(2):
                        total = new[h] + new[2 + h]
                        total = total + turn(total, 127)
                        total = total + turn(total, 112)
                        picked.append(pick(total, mean_index))
                    means[s, j] = 0.125 * jnp.where(mean_low, picked[0], picked[1])
            if done is not None:
                done(i)

    def pack_edge_rate(s):
        for q in range(size_x // 4):
            total = jnp.zeros((8, 128), F32)
            for n in range(4):
                lo = turn(rate8[s, 4 * q + n, :, pl.ds(0, 128)], 16 * n)
                hi = turn(rate8[s, 4 * q + n, :, pl.ds(fine_cols - 128, 128)], 16 * n - 48)
                total = jnp.where(lane8 // 16 == n, lo, total)
                total = jnp.where(lane8 // 16 == 4 + n, hi, total)
            edge_rate[s - 2, q] = total

    edge_index = (lane // 64) * 64 + ((lane % 64) // 32) * 8 + z16 // 2

    def correct(s):
        edge_x, edge_y = ring[0, s, 0], ring[0, s, 1]
        values, rates = [], []
        for side, x in ((0, 0), (1, last)):
            for h in range(2):
                values.append(kappa2 * pick(edge_x, row_index + 64 * side + 32 * h))
                rates.append(wide(rate8[s, x, :, pl.ds(h * 128, 128)]))
        for q in range(size_x // 4):
            values.append(kappa2 * pick(edge_y, edge_index + 16 * q))
            rates.append(wide(edge_rate[s - 2, q]))
        share = chemistry(wf_ref[...], values, rates, F)
        for x in range(size_x):
            q, n = x // 4, x % 4
            both = share[4 + q]
            added = [
                jnp.where(lane < 16, turn(both, -16 * n), 0.0),
                jnp.where(lane >= 112, turn(both, 48 - 16 * n), 0.0),
            ]
            for h in range(2):
                if x == 0:
                    added[h] = added[h] + share[h]
                if x == last:
                    added[h] = added[h] + share[2 + h]
                here = (s, x, slice(None), pl.ds(h * 128, 128))
                buf_b[here] = buf_b[here] + added[h]

    def mid_edges(s):
        return [0.5 * (ring[0, s, side] + ring[1, s, side]) for side in range(2)]

    for s in (2, 3):
        for copy in fine_loads[s]:
            copy.wait()
        spread_rate(s)
        pack_edge_rate(s)
        fine_step(s, 0, None)

    homes = [jnp.full((F, 128), parent_ref[s], jnp.int32) for s in range(slots)]

    def take_ring(level, row):
        turned = turn(row, 64)
        for k in range(2):
            home = homes[k + 2]
            value = ring_recv[level, k, 0]
            value = jnp.where((home == 2) & ~first_half, turned, value)
            value = jnp.where((home == 3) & ~first_half, row, value)
            ring[level, k + 2, 0] = value
            value = ring_recv[level, k, 1]
            if level:
                fix = end_share(cols_new[5])
                added = jnp.where(home == 2, fix[0], jnp.where(home == 3, fix[1], 0.0))
                value = value + added
            ring[level, k + 2, 1] = value

    ring_old.wait_recv()
    take_ring(0, old_row(0))
    for s in (2, 3):
        correct(s)
    ring_new.wait_recv()
    take_ring(1, cnew[0])

    sent = []
    for s in (2, 3):
        def send_part(i, s=s):
            size = size_x // 8
            for m in range(size):
                j = 2 * (size * i + m)
                mean_send[s - 2, i, m] = jnp.where(first_half, means[s, j], means[s, j + 1])
            sent.append(
                send(
                    10 + 2 * (s - 2) + i, mean_send.at[s - 2, i], mean_recv.at[s - 2, i], (left, gy)
                )
            )

        fine_step(s, 1, mid_edges(s), send_part)

    for copy in to_left:
        copy.wait_recv()
    rest = [x for x in range(1, size_x + 1) if x not in (mid - 1, mid)]
    values, rates = [], []
    for at in range(0, len(rest), 2):
        tiles = [row_tile(x) for x in rest[at : at + 2]]
        values += coarse_tiles(tiles)
        rates += [tile[5] for tile in tiles]
    end = jnp.where(lane < 8, from_corner(2, 64, 0), rx[1, near])
    values.append(kappa * jnp.where(lane >= 120, from_corner(3, 0, 120), end))
    end_rate = jnp.where(lane8 < 8, turn(ry[0, rate_rows], 8), crate_row(last))
    rates.append(wide(jnp.where(lane8 >= 120, ry[1, rate_rows], end_rate)))
    result = react(values, rates)
    for x, value in zip(rest[:-1], result):
        cnew[x] = value
    fix = end_share(result[-1])
    tiles_old = ring_tiles([rx[0, near], old_row(mid - 1), old_row(mid), rx[1, near]], old_cols)
    tiles_new = ring_tiles(
        [cols_new[0], cnew[mid - 1], cnew[mid], result[-2]], [cols_new[n] for n in range(1, 5)]
    )
    for p in (2, 3):
        tiles_new[p] = (tiles_new[p][0], tiles_new[p][1] + fix[p - 2])
    for k in range(2):
        for side in range(2):
            ring[0, k, side] = chosen(tiles_old, k, side)
            ring[1, k, side] = chosen(tiles_new, k, side)

    for s in (0, 1):
        for copy in fine_loads[s]:
            copy.wait()
        spread_rate(s)
        fine_step(s, 0, [ring[0, s, 0], ring[0, s, 1]])
        fine_step(s, 1, mid_edges(s))
    for copy in sent:
        copy.wait_recv()

    for x in range(size_x):
        a, X = x // mid, x % mid
        full = [means[0, X], means[1, X]]
        for k in range(2):
            packed = mean_recv[k, X // (mid // 2), (X % (mid // 2)) // 2]
            turned = turn(packed, 64)
            low, high = (packed, turned) if X % 2 == 0 else (turned, packed)
            full.append(jnp.where(first_half, low, high))
        owner = jnp.where(first_half, parents[2 * a], parents[2 * a + 1])
        value = cnew[x]
        for k in range(4):
            value = jnp.where(owner == k, full[k], value)
        cout[pl.ds(x, F, stride=size_x), :] = value
    for copy in to_right + to_side + to_left + [ring_old, ring_new] + sent:
        copy.wait_send()


def store_kernel(cout, fout, coarse_out_hbm, fine_out_hbm, sem):
    copies = [pltpu.make_async_copy(cout, coarse_out_hbm, sem.at[0])]
    slots = fout.shape[0]
    for s in range(slots):
        for h in range(2):
            copies.append(
                pltpu.make_async_copy(
                    fout.at[s, h], fine_out_hbm.at[s, :, pl.ds(h * 128, 128)],
                    sem.at[1 + 2 * s + h],
                )
            )
    for copy in copies:
        copy.start()
    for copy in copies:
        copy.wait()


def body(coarse_state, coarse_rate, fine_state, fine_rate, refine_to, parent_of, kappa, reaction):
    fields, size_x, merged = coarse_state.shape
    slots = fine_state.shape[0]
    fine_merged = fine_state.shape[3]
    flat = fields * size_x
    any_spec = pl.BlockSpec(memory_space=pl.ANY)
    vmem = pl.BlockSpec(memory_space=pltpu.VMEM)
    V = pltpu.VMEM
    tile = (fields, 128)
    cout, fout = pl.pallas_call(
        functools.partial(
            kernel, lax.axis_size("gx"), lax.axis_size("gy"), fields, size_x, slots
        ),
        out_shape=(V((flat, 128), F32), V((slots, 2, flat, 128), F32)),
        in_specs=[any_spec] * 8,
        out_specs=(vmem, vmem),
        scratch_shapes=[
            pltpu.SMEM((slots,), jnp.int32),
            pltpu.SMEM((slots,), jnp.int32),
            V((1, fields), F32),
            V((fields, fields), F32),
            V((flat, 128), F32),
            V((size_x, 128), F32),
            V((slots, 2, flat, 128), F32),
            V((slots, size_x, fine_merged), F32),
            V((slots, size_x, fields, fine_merged), F32),
            V((2, 2 * fields + 8, 128), F32),
            V((2, 2 * fields + 8, 128), F32),
            V((2, 8, 128), F32),
            V((2, 2 * fields + 8, 128), F32),
            V((2, 2 * fields + 8, 128), F32),
            V((4, 8, 128), F32),
            V((size_x,) + tile, F32),
            V((4,) + tile, F32),
            V((2, 8, 128), F32),
            V((2, slots, 2) + tile, F32),
            V((2, 2, 2) + tile, F32),
            V((2, 2, 2) + tile, F32),
            V((slots, size_x // 2) + tile, F32),
            V((2, 2, size_x // 8) + tile, F32),
            V((2, 2, size_x // 8) + tile, F32),
            V((6,) + tile, F32),
            V((4 * fields, 3 * fields), BF16),
            V((4 * fields, 3 * fields), BF16),
            V((slots, size_x, 8, fine_merged), F32),
            V((2, size_x // 4, 8, 128), F32),
            V((256, 256), BF16),
            V((256, 256), BF16),
            pltpu.SemaphoreType.DMA((15,)),
            pltpu.SemaphoreType.DMA((14,)),
            pltpu.SemaphoreType.DMA((14,)),
        ],
        compiler_params=pltpu.CompilerParams(
            collective_id=0, has_side_effects=True, vmem_limit_bytes=24 * 2**20
        ),
    )(
        *[
            pltpu.with_memory_space_constraint(array, pltpu.HBM)
            for array in (
                refine_to, parent_of, coarse_state.reshape(flat, merged), coarse_rate,
                fine_state.reshape(slots, flat, fine_merged), fine_rate,
                kappa.reshape(1, fields), reaction,
            )
        ]
    )
    coarse_out, fine_out = pl.pallas_call(
        store_kernel,
        out_shape=(
            jax.ShapeDtypeStruct((flat, merged), F32),
            jax.ShapeDtypeStruct((slots, flat, fine_merged), F32),
        ),
        in_specs=[vmem, vmem],
        out_specs=(any_spec, any_spec),
        scratch_shapes=[pltpu.SemaphoreType.DMA((1 + 2 * slots,))],
        compiler_params=pltpu.CompilerParams(vmem_limit_bytes=8 * 2**20),
    )(cout, fout)
    return coarse_out.reshape(coarse_state.shape), fine_out.reshape(fine_state.shape)


def solution(mesh):
    in_specs = (
        P(None, "gx", "gy"),
        P("gx", "gy"),
        P(("gx", "gy"), None, None, None),
        P(("gx", "gy"), None, None),
        P(("gx", "gy")),
        P(("gx", "gy")),
        P(),
        P(),
    )
    out_specs = (P(None, "gx", "gy"), P(("gx", "gy"), None, None, None))
    return jax.shard_map(body, mesh=mesh, in_specs=in_specs, out_specs=out_specs, check_vma=False)
```

```python
import functools
import jax
import jax.numpy as jnp
from jax import lax
from jax.experimental import pallas as pl
from jax.experimental.pallas import tpu as pltpu
from jax.sharding import PartitionSpec as P

MESH = pl.DeviceIdType.MESH
F32 = jnp.float32
BF16 = jnp.bfloat16


def lanes(rows):
    return lax.broadcasted_iota(jnp.int32, (rows, 128), 1)


def pick(table, index):
    return jnp.take_along_axis(table, index, axis=1)


def powers(reaction, fields):
    row = lax.broadcasted_iota(jnp.int32, (fields, 3 * fields), 0)
    col = lax.broadcasted_iota(jnp.int32, (fields, 3 * fields), 1)
    power = (col % fields == row).astype(F32)
    result = []
    for _ in range(4):
        power = jnp.dot(
            reaction, power, precision=lax.Precision.HIGHEST, preferred_element_type=F32
        )
        result.append(power)
    return result, col < 2 * fields


def chem_weights(power_list, high_part, step):
    parts = []
    for count, (choose, power) in enumerate(zip((4.0, 6.0, 4.0, 1.0), power_list)):
        value = power * (choose * step ** (count + 1))
        high = value.astype(BF16).astype(F32)
        parts.append(jnp.where(high_part, high, value - high))
    return jnp.concatenate(parts, axis=0).astype(BF16)


def chemistry_product(weights, values):
    wide = jnp.concatenate(values, axis=1)
    high = wide.astype(BF16).astype(F32)
    low = wide - high
    stacked = jnp.concatenate([high, low, high], axis=0).astype(BF16)
    return jnp.dot(weights, stacked, preferred_element_type=F32)


def chemistry_sum(product, values, rates, fields):
    out = []
    for n, (value, rate) in enumerate(zip(values, rates)):
        part = [
            product[q * fields : (q + 1) * fields, n * 128 : (n + 1) * 128] for q in range(4)
        ]
        rate = jnp.broadcast_to(rate, value.shape)
        out.append(value + rate * (part[0] + rate * (part[1] + rate * (part[2] + rate * part[3]))))
    return out


def chemistry(weights, values, rates, fields):
    return chemistry_sum(chemistry_product(weights, values), values, rates, fields)


def shift_matrix(group):
    row = lax.broadcasted_iota(jnp.int32, (256, 128), 0) % 128
    col = lax.broadcasted_iota(jnp.int32, (256, 128), 1)
    same = row // group == col // group
    lower = same & ((col - row + group) % group == 1)
    upper = same & ((row - col + group) % group == 1)
    side = (row - col == group) | (col - row == group)
    around = jnp.where(lower | upper | side, 1.0, 0.0)
    return jnp.concatenate([around, jnp.where(lower, 0.25, 0.0)], axis=1).astype(BF16)


def shifted_sums(matrix, rows):
    high = rows.astype(BF16)
    low = (rows - high.astype(F32)).astype(BF16)
    return jnp.dot(
        jnp.concatenate([high, low], axis=1), matrix, preferred_element_type=F32
    )


def turn(value, shift):
    shift = shift % 128
    return pltpu.roll(value, shift, 1) if shift else value


def kernel(
    n_gx, n_gy, fields, size_x, slots,
    refine_hbm, parent_hbm, coarse_hbm, crate_hbm, fine_hbm, frate_hbm, kappa_hbm, reaction_hbm,
    cout, fout,
    refine_ref, parent_ref, kappa_ref, reaction_ref, cin, crate, fin, frate, buf_b,
    send_r, send_l, col_send, corner_send, rxl, rxr, rx2, ry, rd, rd2, cnew, cols, rate_cols,
    ring, ring_send, ring_recv, means, mean_send, mean_recv,
    cols_new, wf_ref, wc_ref, rate8, edge_rate, shift_f, shift_c,
    in_sem, send_sem, recv_sem, ready_sem,
):
    F = fields
    fine_cols = frate.shape[2]
    last = size_x - 1
    mid = size_x // 2
    gx = lax.axis_index("gx")
    gy = lax.axis_index("gy")
    right = lax.rem(gx + 1, n_gx)
    left = lax.rem(gx + n_gx - 1, n_gx)
    above = lax.rem(gy + 1, n_gy)
    below = lax.rem(gy + n_gy - 1, n_gy)

    barrier = pltpu.get_barrier_semaphore()
    right2 = lax.rem(gx + 2, n_gx)
    left2 = lax.rem(gx + n_gx - 2, n_gx)
    for target in (
        (left, gy), (left, above), (left, below), (gx, above), (gx, below),
        (left2, gy), (left2, above), (left2, below),
    ):
        pl.semaphore_signal(barrier, inc=1, device_id=target, device_id_type=MESH)

    load_coarse = pltpu.make_async_copy(coarse_hbm, cin, in_sem.at[0])
    load_crate = pltpu.make_async_copy(crate_hbm, crate, in_sem.at[1])
    load_frate = pltpu.make_async_copy(frate_hbm, frate, in_sem.at[2])
    fine_loads = [
        [
            pltpu.make_async_copy(
                fine_hbm.at[s, :, pl.ds(h * 128, 128)], fin.at[s, h], in_sem.at[3 + 2 * s + h]
            )
            for h in range(2)
        ]
        for s in range(slots)
    ]
    small = [
        pltpu.make_async_copy(reaction_hbm, reaction_ref, in_sem.at[11]),
        pltpu.make_async_copy(kappa_hbm, kappa_ref, in_sem.at[12]),
        pltpu.make_async_copy(refine_hbm, refine_ref, in_sem.at[13]),
        pltpu.make_async_copy(parent_hbm, parent_ref, in_sem.at[14]),
    ]
    order = (2, 3, 0, 1)
    for copy in [load_coarse, load_crate] + small + [load_frate]:
        copy.start()
    for s in order:
        for copy in fine_loads[s]:
            copy.start()

    def send(n, src, dst, target):
        copy = pltpu.make_async_remote_copy(
            src_ref=src, dst_ref=dst, send_sem=send_sem.at[n], recv_sem=recv_sem.at[n],
            device_id=target, device_id_type=MESH,
        )
        copy.start()
        return copy

    lane = lanes(F)
    lane8 = lanes(8)
    first_half = lane < 64

    shift_f[...] = shift_matrix(16)
    shift_c[...] = shift_matrix(8)

    def pack(rows_of, y, at):
        total = None
        for x in range(size_x):
            moved = turn(rows_of(x), (x - y) * 8)
            total = moved if total is None else jnp.where(at // 8 == x, moved, total)
        return total

    near, far, rate_rows = pl.ds(0, F), pl.ds(F, F), pl.ds(2 * F, 8)
    old_row = lambda x: cin[pl.ds(x, F, stride=size_x), :]
    crate_row = lambda x: jnp.broadcast_to(crate[pl.ds(x, 1), :], (8, 128))

    load_coarse.wait()
    load_crate.wait()
    first_row, first_rate = pl.ds(2 * F + 8, F), pl.ds(3 * F + 8, 8)
    for side, buf, x0, x1 in ((0, send_l, 0, 1), (1, send_r, last, last - 1)):
        row, rate = old_row(x0), crate_row(x0)
        buf[near] = row
        buf[far] = old_row(x1)
        buf[rate_rows] = rate
        pieces = [row[8 * j : 8 * j + 8] for j in range(F // 8)] + [rate]
        if side:
            buf[first_row] = old_row(0)
            buf[first_rate] = crate_row(0)
            pieces.append(crate_row(0))
        corner = pieces[0]
        for j, piece in enumerate(pieces):
            if j:
                corner = jnp.where(lane8 // 8 == j, turn(piece, 8 * j), corner)
            corner = jnp.where(lane8 // 8 == 8 + j, turn(piece, 8 * j - 56), corner)
        corner_send[side] = corner
    for side, (y0, y1) in enumerate(((0, 1), (last, last - 1))):
        col_send[side, near] = pack(old_row, y0, lane)
        col_send[side, far] = pack(old_row, y1, lane)
        col_send[side, rate_rows] = pack(crate_row, y0, lane8)

    for copy in small:
        copy.wait()
    power_list, high_part = powers(reaction_ref[...], F)
    wf_ref[...] = chem_weights(power_list, high_part, 0.125)
    wc_ref[...] = chem_weights(power_list, high_part, 0.25)
    diag = lax.broadcasted_iota(jnp.int32, (F, F), 0) == lax.broadcasted_iota(jnp.int32, (F, F), 1)
    kappa_col = jnp.sum(
        jnp.where(diag, jnp.broadcast_to(kappa_ref[...], (F, F)), 0.0), axis=1, keepdims=True
    )
    kappa = jnp.broadcast_to(kappa_col, (F, 128))
    kappa2 = 2.0 * kappa
    keep_fine = 0.75 - 6.0 * kappa2
    keep_coarse = 0.75 - 6.0 * kappa

    pl.semaphore_wait(barrier, 8)
    to_side = [
        send(2, col_send.at[1], ry.at[0], (gx, above)),
        send(3, col_send.at[0], ry.at[1], (gx, below)),
    ]
    to_right = [
        send(0, send_r, rxl, (right, gy)),
        send(4, corner_send.at[1], rd.at[0], (right, above)),
        send(5, corner_send.at[1], rd.at[1], (right, below)),
        send(14, send_r.at[pl.ds(0, 2 * F + 8)], rx2, (right2, gy)),
        send(15, corner_send.at[1], rd2.at[0], (right2, above)),
        send(16, corner_send.at[1], rd2.at[1], (right2, below)),
    ]
    for target in ((right, gy), (right, above), (right, below)):
        pl.semaphore_signal(ready_sem, inc=1, device_id=target, device_id_type=MESH)
    for n in range(4):
        cols[n] = pack(old_row, mid - 2 + n, lane)
    for n in range(2):
        rate_cols[n] = pack(crate_row, mid - 1 + n, lane8)

    def wide(rate):
        return jnp.concatenate([rate] * (F // 8), axis=0)

    def from_corner(tile, src, dst):
        return jnp.concatenate([turn(tile, dst - src - 8 * j) for j in range(F // 8)], axis=0)

    def coarse_tiles(tiles):
        centers = jnp.concatenate([tile[0] for tile in tiles], axis=0)
        shifted = shifted_sums(shift_c[...], centers)
        values = []
        for n, (center, lo, hi, ghost_lo, ghost_hi, _) in enumerate(tiles):
            part = shifted[F * n : F * n + F]
            lateral = (lo + hi) + part[:, :128]
            if ghost_lo is not None:
                edge = jnp.where(lane >= 120, ghost_hi, 0.0)
                lateral = lateral + jnp.where(lane < 8, ghost_lo, edge)
            values.append(keep_coarse * center + kappa * lateral + part[:, 128:])
        return values

    def react(values, rates):
        out = []
        for at in range(0, len(values), 4):
            out += chemistry(wc_ref[...], values[at : at + 4], rates[at : at + 4], F)
        return out

    def row_tile(x):
        if x == -1:
            return (
                rxl[near], rxl[far], old_row(0),
                from_corner(rd[0], 64, 0), from_corner(rd[1], 0, 120), wide(rxl[rate_rows]),
            )
        if x == size_x:
            return (
                rxr[near], old_row(last), rxr[far],
                from_corner(rd[2], 64, 0), from_corner(rd[3], 0, 120), wide(rxr[rate_rows]),
            )
        return (
            old_row(x),
            old_row(x - 1) if x else rxl[near],
            old_row(x + 1) if x < last else rxr[near],
            turn(ry[0, near], -8 * x), turn(ry[1, near], 120 - 8 * x),
            crate[pl.ds(x, 1), :],
        )

    def extended(row, lo, hi, at=None):
        at = lane if at is None else at
        return jnp.where(at < 8, lo, jnp.where(at >= 120, hi, row))

    def joined(lo, hi, half):
        if half == 0:
            return jnp.where(first_half, lo, turn(hi, 64))
        return jnp.where(first_half, turn(lo, 64), hi)

    parents = [jnp.full((F, 128), refine_ref[p], jnp.int32) for p in range(4)]

    def ring_tiles(row_at, col_at):
        return [
            (
                joined(row_at[p // 2], row_at[p // 2 + 2], p % 2),
                joined(col_at[p % 2], col_at[p % 2 + 2], p // 2),
            )
            for p in range(4)
        ]

    def chosen(tiles, k, side):
        value = jnp.zeros((F, 128), F32)
        for p in range(4):
            value = jnp.where(parents[p] == k, tiles[p][side], value)
        return value

    def send_ring(level, low_row, high_row, col_at):
        tiles = ring_tiles([low_row] * 4, col_at)
        halves = []
        for k in range(2):
            value = jnp.zeros((F, 128), F32)
            for p in range(4):
                row = low_row if p // 2 else high_row
                row = row if p % 2 == k else turn(row, 64)
                value = jnp.where(parents[p] == k + 2, row, value)
            halves.append(value)
            ring_send[level, 1 + k] = chosen(tiles, k + 2, 1)
        ring_send[level, 0] = jnp.where(first_half, halves[0], halves[1])
        return send(8 + level, ring_send.at[level], ring_recv.at[level], (right, gy))

    group = lane // 8

    def end_shares(before, after):
        at_first = (group == 0) | (group == 8)
        at_last = (group == 7) | (group == 15)
        return [
            jnp.where(at_first, before, 0.0), jnp.where(at_first, turn(before, 72), 0.0),
            jnp.where(at_last, turn(after, 56), 0.0), jnp.where(at_last, after, 0.0),
        ]

    for copy in to_side:
        copy.wait_recv()
    old_cols = [ry[0, near], cols[1], cols[2], ry[1, near]]
    ring_old = send_ring(0, old_row(mid - 1), old_row(mid), old_cols)
    tiles = [
        row_tile(mid - 1), row_tile(mid),
        (ry[0, near], ry[0, far], col_send[0, near], None, None, wide(ry[0, rate_rows])),
        (cols[1], cols[0], cols[2], None, None, wide(rate_cols[0])),
        (cols[2], cols[1], cols[3], None, None, wide(rate_cols[1])),
        (ry[1, near], col_send[1, near], ry[1, far], None, None, wide(ry[1, rate_rows])),
    ]
    result = react(coarse_tiles(tiles), [tile[5] for tile in tiles])
    cnew[mid - 1], cnew[mid] = result[:2]
    for n in range(4):
        cols_new[n] = result[2 + n]
    ring_new = send_ring(1, result[0], result[1], result[2:])

    pl.semaphore_wait(ready_sem, 3)
    to_left = [
        send(1, send_l, rxr, (left, gy)),
        send(6, corner_send.at[0], rd.at[2], (left, above)),
        send(7, corner_send.at[0], rd.at[3], (left, below)),
    ]

    z16 = lane % 16
    row_index = (lane // 32) * 8 + z16 // 2
    col_index = jnp.where(lane < 64, 0, 64) + z16 // 2
    target = lane % 64
    mean_index = ((target // 8) % 4) * 32 + 2 * (target % 8)
    mean_low = target // 32 == 0
    edge_lane = (lane < 16) | (lane >= 112)

    load_frate.wait()

    chunk = 8

    def spread_rate(s):
        for x in range(size_x):
            rate8[s, x] = jnp.broadcast_to(frate[s, pl.ds(x, 1), :], rate8.shape[2:])

    def fine_jobs(s, step, get_edges, done=None):
        state = {}

        def edges_of():
            if "edges" not in state:
                state["edges"] = get_edges() if get_edges else None
            return state["edges"]

        def row_of(x, h):
            if 0 <= x < size_x:
                if step == 0:
                    return fin[s, h, pl.ds(x, F, stride=size_x), :]
                return buf_b[s, x, :, pl.ds(h * 128, 128)]
            edges = edges_of()
            if edges is None:
                return None
            return pick(edges[0], row_index + 32 * h + (64 if x > 0 else 0))

        def shift_part(i):
            span = range(chunk * i - 1, chunk * i + chunk + 1)
            rows = [[row_of(x, h) for h in range(2)] for x in span]
            state[i] = rows, shifted_sums(
                shift_f[...], jnp.concatenate([v for row in rows[1:-1] for v in row], axis=0)
            )

        def product_part(j):
            edges = edges_of()
            i, m = 2 * j // chunk, j % (chunk // 2)
            rows, shifted = state[i]
            if edges is None:
                ghost = 0.0
            else:
                ghost = jnp.where(edge_lane, pick(edges[1], col_index + 8 * j), 0.0)
            values = []
            for n in range(2):
                r = 2 * m + n + 1
                v0, v1 = rows[r]
                cross = [
                    jnp.where(lane >= 112, turn(v1, 112), ghost),
                    jnp.where(lane < 16, turn(v0, 16), ghost),
                ]
                for h in range(2):
                    at = F * (2 * (r - 1) + h)
                    part = shifted[at : at + F]
                    lateral = part[:, :128] + cross[h]
                    for near_row in (rows[r - 1][h], rows[r + 1][h]):
                        if near_row is not None:
                            lateral = lateral + near_row
                    values.append(keep_fine * rows[r][h] + kappa2 * lateral + part[:, 128:])
            state["p", j] = values, chemistry_product(wf_ref[...], values)

        def sum_part(j):
            values, product = state.pop(("p", j))
            rates = [
                wide(rate8[s, 2 * j + n, :, pl.ds(h * 128, 128)])
                for n in range(2) for h in range(2)
            ]
            new = chemistry_sum(product, values, rates, F)
            if step == 0:
                for n in range(2):
                    for h in range(2):
                        buf_b[s, 2 * j + n, :, pl.ds(h * 128, 128)] = new[2 * n + h]
            else:
                live = jnp.full((F, 128), parent_ref[s], jnp.int32) >= 0
                new = [jnp.where(live, v, 0.0) for v in new]
                for n in range(2):
                    for h in range(2):
                        fout[s, h, pl.ds(2 * j + n, F, stride=size_x), :] = new[2 * n + h]
                picked = []
                for h in range(2):
                    total = new[h] + new[2 + h]
                    total = total + turn(total, 127)
                    total = total + turn(total, 112)
                    picked.append(pick(total, mean_index))
                means[s, j] = 0.125 * jnp.where(mean_low, picked[0], picked[1])
            if done is not None:
                done(j)

        pairs = size_x // 2
        return [
            (
                functools.partial(shift_part, 2 * j // chunk) if 2 * j % chunk == 0 else None,
                functools.partial(product_part, j), functools.partial(sum_part, j),
            )
            for j in range(pairs)
        ]

    def run(jobs):
        lead, lag = 4, 2
        for n in range(-lead, len(jobs) + lag):
            if n + lead < len(jobs) and jobs[n + lead][0] is not None:
                jobs[n + lead][0]()
            if 0 <= n < len(jobs):
                jobs[n][1]()
            if n >= lag:
                jobs[n - lag][2]()

    def pack_edge_rate(s):
        for q in range(size_x // 4):
            total = jnp.zeros((8, 128), F32)
            for n in range(4):
                lo = turn(rate8[s, 4 * q + n, :, pl.ds(0, 128)], 16 * n)
                hi = turn(rate8[s, 4 * q + n, :, pl.ds(fine_cols - 128, 128)], 16 * n - 48)
                total = jnp.where(lane8 // 16 == n, lo, total)
                total = jnp.where(lane8 // 16 == 4 + n, hi, total)
            edge_rate[s, q] = total

    edge_index = (lane // 64) * 64 + ((lane % 64) // 32) * 8 + z16 // 2

    def correct(s):
        edge_x, edge_y = ring[0, s, 0], ring[0, s, 1]
        values, rates = [], []
        for side, x in ((0, 0), (1, last)):
            for h in range(2):
                values.append(kappa2 * pick(edge_x, row_index + 64 * side + 32 * h))
                rates.append(wide(rate8[s, x, :, pl.ds(h * 128, 128)]))
        for q in range(size_x // 4):
            values.append(kappa2 * pick(edge_y, edge_index + 16 * q))
            rates.append(wide(edge_rate[s, q]))
        share = chemistry(wf_ref[...], values, rates, F)
        for x in range(size_x):
            q, n = x // 4, x % 4
            both = share[4 + q]
            added = [
                jnp.where(lane < 16, turn(both, -16 * n), 0.0),
                jnp.where(lane >= 112, turn(both, 48 - 16 * n), 0.0),
            ]
            for h in range(2):
                if x == 0:
                    added[h] = added[h] + share[h]
                if x == last:
                    added[h] = added[h] + share[2 + h]
                here = (s, x, slice(None), pl.ds(h * 128, 128))
                buf_b[here] = buf_b[here] + added[h]

    def mid_edges(s):
        return [0.5 * (ring[0, s, side] + ring[1, s, side]) for side in range(2)]

    for s in order:
        for copy in fine_loads[s]:
            copy.wait()
    for s in order:
        spread_rate(s)
        pack_edge_rate(s)
    run([job for s in order for job in fine_jobs(s, 0, None)])

    homes = [jnp.full((F, 128), parent_ref[s], jnp.int32) for s in range(slots)]

    def fill_rows(rows):
        for at in range(0, len(rows), 4):
            tiles = [row_tile(x) for x in rows[at : at + 4]]
            result = react(coarse_tiles(tiles), [tile[5] for tile in tiles])
            for x, value in zip(rows[at : at + 4], result):
                cnew[x] = value

    fill_rows([x for x in range(1, last) if x not in (mid - 1, mid)])

    for copy in to_right:
        copy.wait_recv()
    tiles = [
        row_tile(-1), row_tile(0),
        (
            rx2[near], rx2[far], rxl[first_row],
            from_corner(rd2[0], 64, 0), from_corner(rd2[1], 0, 120), wide(rx2[rate_rows]),
        ),
    ]
    values = coarse_tiles(tiles)
    rates = [tile[5] for tile in tiles]
    values.append(
        kappa * extended(old_row(0), ry[0, near], turn(ry[1, near], 120))
    )
    rates.append(wide(extended(rxl[rate_rows], turn(rd[0], 40), turn(rd[1], 96), lane8)))
    values.append(kappa * extended(rx2[near], tiles[2][3], tiles[2][4]))
    rates.append(wide(extended(rxl[first_rate], turn(rd[0], 32), turn(rd[1], 88), lane8)))
    values.append(kappa * extended(rxl[near], tiles[0][3], tiles[0][4]))
    rates.append(
        wide(extended(crate_row(0), ry[0, rate_rows], turn(ry[1, rate_rows], 120), lane8))
    )
    result = react(values, rates)
    cnew[0] = result[1]
    for n, value in zip(range(4, 9), (result[0], result[2], result[3], result[4], result[5])):
        cols_new[n] = value

    def take_ring(level):
        before = cols_new[5] if level else rx2[near]
        after = cnew[0] if level else old_row(0)
        fix = end_shares(cols_new[7], cols_new[6]) if level else None
        shared = ring_recv[level, 0]
        turned = turn(shared, 64)
        for k in range(2):
            home = homes[k + 2]
            low, high = (shared, turned) if k == 0 else (turned, shared)
            kinds = [
                jnp.where(first_half, before, high), jnp.where(first_half, turn(before, 64), high),
                jnp.where(first_half, low, turn(after, 64)), jnp.where(first_half, low, after),
            ]
            value, added = kinds[3], fix[3] if level else None
            for p in range(3):
                value = jnp.where(home == p, kinds[p], value)
                if level:
                    added = jnp.where(home == p, fix[p], added)
            ring[level, k + 2, 0] = value
            value = ring_recv[level, 1 + k]
            ring[level, k + 2, 1] = value + added if level else value

    def local_part():
        for copy in to_left:
            copy.wait_recv()
        tiles = [row_tile(last), row_tile(size_x)]
        values = coarse_tiles(tiles)
        values.append(
            kappa * extended(rxr[near], from_corner(rd[2], 64, 0), from_corner(rd[3], 0, 120))
        )
        rate = extended(crate_row(last), turn(ry[0, rate_rows], 8), ry[1, rate_rows], lane8)
        result = react(values, [tile[5] for tile in tiles] + [wide(rate)])
        cnew[last] = result[0]
        fix = end_shares(cols_new[8], result[2])
        tiles_old = ring_tiles(
            [rxl[near], old_row(mid - 1), old_row(mid), rxr[near]],
            [ry[0, near], cols[1], cols[2], ry[1, near]],
        )
        tiles_new = ring_tiles(
            [cols_new[4], cnew[mid - 1], cnew[mid], result[1]], [cols_new[n] for n in range(4)]
        )
        tiles_new = [(tile[0], tile[1] + fix[p]) for p, tile in enumerate(tiles_new)]
        for k in range(2):
            for side in range(2):
                ring[0, k, side] = chosen(tiles_old, k, side)
                ring[1, k, side] = chosen(tiles_new, k, side)
        for s in (0, 1):
            correct(s)
        run(
            [
                job for s in (0, 1)
                for job in fine_jobs(s, 1, functools.partial(mid_edges, s))
            ]
        )

    @pl.when(gx == 0)
    def _():
        local_part()

    ring_old.wait_recv()
    take_ring(0)
    for s in (2, 3):
        correct(s)
    ring_new.wait_recv()
    take_ring(1)

    sent, jobs = [], []
    for s in (2, 3):
        def send_part(i, s=s):
            size = size_x // 8
            if 4 * (i + 1) % size_x:
                return
            i = 4 * i // size_x
            for m in range(size):
                j = 2 * (size * i + m)
                mean_send[s - 2, i, m] = jnp.where(first_half, means[s, j], means[s, j + 1])
            sent.append(
                send(
                    10 + 2 * (s - 2) + i, mean_send.at[s - 2, i], mean_recv.at[s - 2, i], (left, gy)
                )
            )

        jobs += fine_jobs(s, 1, functools.partial(mid_edges, s), send_part)
    run(jobs)

    @pl.when(gx != 0)
    def _():
        local_part()

    for copy in sent:
        copy.wait_recv()

    for x in range(size_x):
        a, X = x // mid, x % mid
        full = [means[0, X], means[1, X]]
        for k in range(2):
            packed = mean_recv[k, X // (mid // 2), (X % (mid // 2)) // 2]
            turned = turn(packed, 64)
            low, high = (packed, turned) if X % 2 == 0 else (turned, packed)
            full.append(jnp.where(first_half, low, high))
        owner = jnp.where(first_half, parents[2 * a], parents[2 * a + 1])
        value = cnew[x]
        for k in range(4):
            value = jnp.where(owner == k, full[k], value)
        cout[pl.ds(x, F, stride=size_x), :] = value
    for copy in to_right + to_side + to_left + [ring_old, ring_new] + sent:
        copy.wait_send()


def store_kernel(cout, fout, coarse_out_hbm, fine_out_hbm, sem):
    copies = [pltpu.make_async_copy(cout, coarse_out_hbm, sem.at[0])]
    slots = fout.shape[0]
    for s in range(slots):
        for h in range(2):
            copies.append(
                pltpu.make_async_copy(
                    fout.at[s, h], fine_out_hbm.at[s, :, pl.ds(h * 128, 128)],
                    sem.at[1 + 2 * s + h],
                )
            )
    for copy in copies:
        copy.start()
    for copy in copies:
        copy.wait()


def body(coarse_state, coarse_rate, fine_state, fine_rate, refine_to, parent_of, kappa, reaction):
    fields, size_x, merged = coarse_state.shape
    slots = fine_state.shape[0]
    fine_merged = fine_state.shape[3]
    flat = fields * size_x
    any_spec = pl.BlockSpec(memory_space=pl.ANY)
    vmem = pl.BlockSpec(memory_space=pltpu.VMEM)
    V = pltpu.VMEM
    tile = (fields, 128)
    cout, fout = pl.pallas_call(
        functools.partial(
            kernel, lax.axis_size("gx"), lax.axis_size("gy"), fields, size_x, slots
        ),
        out_shape=(V((flat, 128), F32), V((slots, 2, flat, 128), F32)),
        in_specs=[any_spec] * 8,
        out_specs=(vmem, vmem),
        scratch_shapes=[
            pltpu.SMEM((slots,), jnp.int32),
            pltpu.SMEM((slots,), jnp.int32),
            V((1, fields), F32),
            V((fields, fields), F32),
            V((flat, 128), F32),
            V((size_x, 128), F32),
            V((slots, 2, flat, 128), F32),
            V((slots, size_x, fine_merged), F32),
            V((slots, size_x, fields, fine_merged), F32),
            V((3 * fields + 16, 128), F32),
            V((2 * fields + 8, 128), F32),
            V((2, 2 * fields + 8, 128), F32),
            V((2, 8, 128), F32),
            V((3 * fields + 16, 128), F32),
            V((2 * fields + 8, 128), F32),
            V((2 * fields + 8, 128), F32),
            V((2, 2 * fields + 8, 128), F32),
            V((4, 8, 128), F32),
            V((2, 8, 128), F32),
            V((size_x,) + tile, F32),
            V((4,) + tile, F32),
            V((2, 8, 128), F32),
            V((2, slots, 2) + tile, F32),
            V((2, 3) + tile, F32),
            V((2, 3) + tile, F32),
            V((slots, size_x // 2) + tile, F32),
            V((2, 2, size_x // 8) + tile, F32),
            V((2, 2, size_x // 8) + tile, F32),
            V((9,) + tile, F32),
            V((4 * fields, 3 * fields), BF16),
            V((4 * fields, 3 * fields), BF16),
            V((slots, size_x, 8, fine_merged), F32),
            V((slots, size_x // 4, 8, 128), F32),
            V((256, 256), BF16),
            V((256, 256), BF16),
            pltpu.SemaphoreType.DMA((15,)),
            pltpu.SemaphoreType.DMA((17,)),
            pltpu.SemaphoreType.DMA((17,)),
            pltpu.SemaphoreType.REGULAR,
        ],
        compiler_params=pltpu.CompilerParams(
            collective_id=0, has_side_effects=True, vmem_limit_bytes=24 * 2**20
        ),
    )(
        *[
            pltpu.with_memory_space_constraint(array, pltpu.HBM)
            for array in (
                refine_to, parent_of, coarse_state.reshape(flat, merged), coarse_rate,
                fine_state.reshape(slots, flat, fine_merged), fine_rate,
                kappa.reshape(1, fields), reaction,
            )
        ]
    )
    coarse_out, fine_out = pl.pallas_call(
        store_kernel,
        out_shape=(
            jax.ShapeDtypeStruct((flat, merged), F32),
            jax.ShapeDtypeStruct((slots, flat, fine_merged), F32),
        ),
        in_specs=[vmem, vmem],
        out_specs=(any_spec, any_spec),
        scratch_shapes=[pltpu.SemaphoreType.DMA((1 + 2 * slots,))],
        compiler_params=pltpu.CompilerParams(vmem_limit_bytes=8 * 2**20),
    )(cout, fout)
    return coarse_out.reshape(coarse_state.shape), fine_out.reshape(fine_state.shape)


def solution(mesh):
    in_specs = (
        P(None, "gx", "gy"),
        P("gx", "gy"),
        P(("gx", "gy"), None, None, None),
        P(("gx", "gy"), None, None),
        P(("gx", "gy")),
        P(("gx", "gy")),
        P(),
        P(),
    )
    out_specs = (P(None, "gx", "gy"), P(("gx", "gy"), None, None, None))
    return jax.shard_map(body, mesh=mesh, in_specs=in_specs, out_specs=out_specs, check_vma=False)
```

```python
import functools
import jax
import jax.numpy as jnp
from jax import lax
from jax.experimental import pallas as pl
from jax.experimental.pallas import tpu as pltpu
from jax.sharding import PartitionSpec as P

MESH = pl.DeviceIdType.MESH
F32 = jnp.float32
BF16 = jnp.bfloat16


def lanes(rows):
    return lax.broadcasted_iota(jnp.int32, (rows, 128), 1)


def pick(table, index):
    return jnp.take_along_axis(table, index, axis=1)


def powers(reaction, fields):
    row = lax.broadcasted_iota(jnp.int32, (fields, 3 * fields), 0)
    col = lax.broadcasted_iota(jnp.int32, (fields, 3 * fields), 1)
    power = (col % fields == row).astype(F32)
    result = []
    for _ in range(4):
        power = jnp.dot(
            reaction, power, precision=lax.Precision.HIGHEST, preferred_element_type=F32
        )
        result.append(power)
    return result, col < 2 * fields


def chem_weights(power_list, high_part, step):
    parts = []
    for count, (choose, power) in enumerate(zip((4.0, 6.0, 4.0, 1.0), power_list)):
        value = power * (choose * step ** (count + 1))
        high = value.astype(BF16).astype(F32)
        parts.append(jnp.where(high_part, high, value - high))
    return jnp.concatenate(parts, axis=0).astype(BF16)


def chemistry_product(weights, values):
    wide = jnp.concatenate(values, axis=1)
    high = wide.astype(BF16).astype(F32)
    low = wide - high
    stacked = jnp.concatenate([high, low, high], axis=0).astype(BF16)
    return jnp.dot(weights, stacked, preferred_element_type=F32)


def chemistry_sum(product, values, rates, fields):
    out = []
    for n, (value, rate) in enumerate(zip(values, rates)):
        part = [
            product[q * fields : (q + 1) * fields, n * 128 : (n + 1) * 128] for q in range(4)
        ]
        rate = jnp.broadcast_to(rate, value.shape)
        out.append(value + rate * (part[0] + rate * (part[1] + rate * (part[2] + rate * part[3]))))
    return out


def chemistry(weights, values, rates, fields):
    return chemistry_sum(chemistry_product(weights, values), values, rates, fields)


def shift_matrix(group):
    row = lax.broadcasted_iota(jnp.int32, (256, 128), 0) % 128
    col = lax.broadcasted_iota(jnp.int32, (256, 128), 1)
    same = row // group == col // group
    lower = same & ((col - row + group) % group == 1)
    upper = same & ((row - col + group) % group == 1)
    side = (row - col == group) | (col - row == group)
    around = jnp.where(lower | upper | side, 1.0, 0.0)
    return jnp.concatenate([around, jnp.where(lower, 0.25, 0.0)], axis=1).astype(BF16)


def shifted_sums(matrix, rows):
    high = rows.astype(BF16)
    low = (rows - high.astype(F32)).astype(BF16)
    return jnp.dot(
        jnp.concatenate([high, low], axis=1), matrix, preferred_element_type=F32
    )


def turn(value, shift):
    shift = shift % 128
    return pltpu.roll(value, shift, 1) if shift else value


def kernel(
    n_gx, n_gy, fields, size_x, slots,
    refine_hbm, parent_hbm, coarse_hbm, crate_hbm, fine_hbm, frate_hbm, kappa_hbm, reaction_hbm,
    cout, fout,
    refine_ref, parent_ref, kappa_ref, reaction_ref, cin, crate, fin, frate, buf_b,
    send_r, send_l, col_send, corner_send, rxl, rxr, rx2, ry, rd, rd2, cnew, cols, rate_cols,
    ring, ring_send, ring_recv, means, mean_send, mean_recv,
    cols_new, wf_ref, wc_ref, rate8, edge_rate, shift_f, shift_c,
    in_sem, send_sem, recv_sem, ready_sem,
):
    F = fields
    fine_cols = frate.shape[2]
    last = size_x - 1
    mid = size_x // 2
    gx = lax.axis_index("gx")
    gy = lax.axis_index("gy")
    right = lax.rem(gx + 1, n_gx)
    left = lax.rem(gx + n_gx - 1, n_gx)
    above = lax.rem(gy + 1, n_gy)
    below = lax.rem(gy + n_gy - 1, n_gy)

    barrier = pltpu.get_barrier_semaphore()
    right2 = lax.rem(gx + 2, n_gx)
    left2 = lax.rem(gx + n_gx - 2, n_gx)
    sides = [above] if n_gy == 2 else [above, below]
    targets = [(x, y) for x in (left, left2) for y in [gy] + sides] + [(gx, y) for y in sides]
    for target in targets:
        pl.semaphore_signal(barrier, inc=1, device_id=target, device_id_type=MESH)

    load_coarse = pltpu.make_async_copy(coarse_hbm, cin, in_sem.at[0])
    load_crate = pltpu.make_async_copy(crate_hbm, crate, in_sem.at[1])
    load_frate = pltpu.make_async_copy(frate_hbm, frate, in_sem.at[2])
    fine_loads = [
        [
            pltpu.make_async_copy(
                fine_hbm.at[s, :, pl.ds(h * 128, 128)], fin.at[s, h], in_sem.at[3 + 2 * s + h]
            )
            for h in range(2)
        ]
        for s in range(slots)
    ]
    small = [
        pltpu.make_async_copy(reaction_hbm, reaction_ref, in_sem.at[11]),
        pltpu.make_async_copy(kappa_hbm, kappa_ref, in_sem.at[12]),
        pltpu.make_async_copy(refine_hbm, refine_ref, in_sem.at[13]),
        pltpu.make_async_copy(parent_hbm, parent_ref, in_sem.at[14]),
    ]
    order = (2, 3, 0, 1)
    for copy in [load_coarse, load_crate] + small + [load_frate]:
        copy.start()
    for s in order:
        for copy in fine_loads[s]:
            copy.start()

    def send(n, src, dst, target):
        copy = pltpu.make_async_remote_copy(
            src_ref=src, dst_ref=dst, send_sem=send_sem.at[n], recv_sem=recv_sem.at[n],
            device_id=target, device_id_type=MESH,
        )
        copy.start()
        return copy

    lane = lanes(F)
    lane8 = lanes(8)
    first_half = lane < 64

    near, far, rate_rows = pl.ds(0, F), pl.ds(F, F), pl.ds(2 * F, 8)
    old_row = lambda x: cin[pl.ds(x, F, stride=size_x), :]
    crate_row = lambda x: jnp.broadcast_to(crate[pl.ds(x, 1), :], (8, 128))

    load_coarse.wait()
    load_crate.wait()
    first_row, first_rate = pl.ds(2 * F + 8, F), pl.ds(3 * F + 8, 8)
    def fill_row_message(side, buf, x0, x1):
        row, rate = old_row(x0), crate_row(x0)
        buf[near] = row
        buf[far] = old_row(x1)
        buf[rate_rows] = rate
        pieces = [row[8 * j : 8 * j + 8] for j in range(F // 8)] + [rate]
        if side:
            buf[first_row] = old_row(0)
            buf[first_rate] = crate_row(0)
            pieces.append(crate_row(0))
        corner = pieces[0]
        for j, piece in enumerate(pieces):
            if j:
                corner = jnp.where(lane8 // 8 == j, turn(piece, 8 * j), corner)
            corner = jnp.where(lane8 // 8 == 8 + j, turn(piece, 8 * j - 56), corner)
        corner_send[side] = corner
    fill_row_message(1, send_r, last, last - 1)
    pl.semaphore_wait(barrier, len(targets))
    to_right = [
        send(0, send_r, rxl, (right, gy)),
        send(14, send_r.at[pl.ds(0, 2 * F + 8)], rx2, (right2, gy)),
    ]
    to_right1, to_right2 = to_right[:1], to_right[1:]
    for n, y in enumerate(sides):
        to_right1.append(send(4 + n, corner_send.at[1], rd.at[n], (right, y)))
        to_right2.append(send(15 + n, corner_send.at[1], rd2.at[n], (right2, y)))
    to_right = to_right1 + to_right2
    for y in [gy] + sides:
        pl.semaphore_signal(ready_sem, inc=1, device_id=(right, y), device_id_type=MESH)

    group32 = lanes(F + 8) // 8
    columns = {
        x: jnp.concatenate([old_row(x), crate_row(x)], axis=0) for x in range(size_x)
    }
    wanted = (0, 1, mid - 2, mid - 1, mid, mid + 1, last - 1, last)
    bits = [size_x // 8, size_x // 4, 1, size_x // 2]
    for n, bit in enumerate(bits):
        free = sum(bits[n + 1 :])
        moved = {}
        for x in range(size_x):
            if any((x ^ y) & ~free == 0 for y in wanted):
                other = columns[x ^ bit]
                lower = group32 & bit == 0
                if x & bit:
                    moved[x] = jnp.where(lower, turn(other, -8 * bit), columns[x])
                else:
                    moved[x] = jnp.where(lower, columns[x], turn(other, 8 * bit))
        columns = moved
    for side, (y0, y1) in enumerate(((0, 1), (last, last - 1))):
        col_send[side, near] = columns[y0][:F]
        col_send[side, far] = columns[y1][:F]
        col_send[side, rate_rows] = columns[y0][F:]
    to_side = [
        send(2, col_send.at[1], ry.at[0], (gx, above)),
        send(3, col_send.at[0], ry.at[1], (gx, below)),
    ]
    for n in range(4):
        cols[n] = columns[mid - 2 + n][:F]
    for n in range(2):
        rate_cols[n] = columns[mid - 1 + n][F:]

    for copy in small:
        copy.wait()
    power_list, high_part = powers(reaction_ref[...], F)
    wf_ref[...] = chem_weights(power_list, high_part, 0.125)
    wc_ref[...] = chem_weights(power_list, high_part, 0.25)
    diag = lax.broadcasted_iota(jnp.int32, (F, F), 0) == lax.broadcasted_iota(jnp.int32, (F, F), 1)
    kappa_col = jnp.sum(
        jnp.where(diag, jnp.broadcast_to(kappa_ref[...], (F, F)), 0.0), axis=1, keepdims=True
    )
    kappa = jnp.broadcast_to(kappa_col, (F, 128))
    kappa2 = 2.0 * kappa
    keep_fine = 0.75 - 6.0 * kappa2
    keep_coarse = 0.75 - 6.0 * kappa
    shift_c[...] = shift_matrix(8)
    fill_row_message(0, send_l, 0, 1)
    corners = [rd.at[n] for n in ((0, 0, 2, 2) if n_gy == 2 else (0, 1, 2, 3))]
    corners2 = [rd2.at[n] for n in ((0, 0) if n_gy == 2 else (0, 1))]

    def wide(rate):
        return jnp.concatenate([rate] * (F // 8), axis=0)

    def from_corner(tile, src, dst):
        return jnp.concatenate([turn(tile, dst - src - 8 * j) for j in range(F // 8)], axis=0)

    def coarse_tiles(tiles):
        centers = jnp.concatenate([tile[0] for tile in tiles], axis=0)
        shifted = shifted_sums(shift_c[...], centers)
        values = []
        for n, (center, lo, hi, ghost_lo, ghost_hi, _) in enumerate(tiles):
            part = shifted[F * n : F * n + F]
            lateral = (lo + hi) + part[:, :128]
            if ghost_lo is not None:
                edge = jnp.where(lane >= 120, ghost_hi, 0.0)
                lateral = lateral + jnp.where(lane < 8, ghost_lo, edge)
            values.append(keep_coarse * center + kappa * lateral + part[:, 128:])
        return values

    def react(values, rates):
        out = []
        for at in range(0, len(values), 4):
            out += chemistry(wc_ref[...], values[at : at + 4], rates[at : at + 4], F)
        return out

    def row_tile(x):
        if x == -1:
            return (
                rxl[near], rxl[far], old_row(0),
                from_corner(corners[0][...], 64, 0), from_corner(corners[1][...], 0, 120), wide(rxl[rate_rows]),
            )
        if x == size_x:
            return (
                rxr[near], old_row(last), rxr[far],
                from_corner(corners[2][...], 64, 0), from_corner(corners[3][...], 0, 120), wide(rxr[rate_rows]),
            )
        return (
            old_row(x),
            old_row(x - 1) if x else rxl[near],
            old_row(x + 1) if x < last else rxr[near],
            turn(ry[0, near], -8 * x), turn(ry[1, near], 120 - 8 * x),
            crate[pl.ds(x, 1), :],
        )

    def extended(row, lo, hi, at=None):
        at = lane if at is None else at
        return jnp.where(at < 8, lo, jnp.where(at >= 120, hi, row))

    def joined(lo, hi, half):
        if half == 0:
            return jnp.where(first_half, lo, turn(hi, 64))
        return jnp.where(first_half, turn(lo, 64), hi)

    parents = [jnp.full((F, 128), refine_ref[p], jnp.int32) for p in range(4)]

    def ring_tiles(row_at, col_at):
        return [
            (
                joined(row_at[p // 2], row_at[p // 2 + 2], p % 2),
                joined(col_at[p % 2], col_at[p % 2 + 2], p // 2),
            )
            for p in range(4)
        ]

    def chosen(tiles, k, side):
        value = jnp.zeros((F, 128), F32)
        for p in range(4):
            value = jnp.where(parents[p] == k, tiles[p][side], value)
        return value

    def send_ring(level, low_row, high_row, col_at):
        tiles = ring_tiles([low_row] * 4, col_at)
        halves = []
        for k in range(2):
            value = jnp.zeros((F, 128), F32)
            for p in range(4):
                row = low_row if p // 2 else high_row
                row = row if p % 2 == k else turn(row, 64)
                value = jnp.where(parents[p] == k + 2, row, value)
            halves.append(value)
            ring_send[level, 1 + k] = chosen(tiles, k + 2, 1)
        ring_send[level, 0] = jnp.where(first_half, halves[0], halves[1])
        return send(8 + level, ring_send.at[level], ring_recv.at[level], (right, gy))

    group = lane // 8

    def end_shares(before, after):
        at_first = (group == 0) | (group == 8)
        at_last = (group == 7) | (group == 15)
        return [
            jnp.where(at_first, before, 0.0), jnp.where(at_first, turn(before, 72), 0.0),
            jnp.where(at_last, turn(after, 56), 0.0), jnp.where(at_last, after, 0.0),
        ]

    for copy in to_side:
        copy.wait_recv()
    old_cols = [ry[0, near], cols[1], cols[2], ry[1, near]]
    ring_old = send_ring(0, old_row(mid - 1), old_row(mid), old_cols)
    tiles = [
        row_tile(mid - 1), row_tile(mid),
        (ry[0, near], ry[0, far], col_send[0, near], None, None, wide(ry[0, rate_rows])),
        (cols[1], cols[0], cols[2], None, None, wide(rate_cols[0])),
        (cols[2], cols[1], cols[3], None, None, wide(rate_cols[1])),
        (ry[1, near], col_send[1, near], ry[1, far], None, None, wide(ry[1, rate_rows])),
    ]
    result = react(coarse_tiles(tiles), [tile[5] for tile in tiles])
    cnew[mid - 1], cnew[mid] = result[:2]
    for n in range(4):
        cols_new[n] = result[2 + n]
    ring_new = send_ring(1, result[0], result[1], result[2:])

    shift_f[...] = shift_matrix(16)
    z16 = lane % 16
    row_index = (lane // 32) * 8 + z16 // 2
    col_index = jnp.where(lane < 64, 0, 64) + z16 // 2
    target = lane % 64
    mean_index = ((target // 8) % 4) * 32 + 2 * (target % 8)
    mean_low = target // 32 == 0
    edge_lane = (lane < 16) | (lane >= 112)

    load_frate.wait()

    chunk = 8

    def spread_rate(s):
        for x in range(size_x):
            rate8[s, x] = jnp.broadcast_to(frate[s, pl.ds(x, 1), :], rate8.shape[2:])

    def fine_jobs(s, step, get_edges, done=None):
        state = {}

        def edges_of():
            if "edges" not in state:
                state["edges"] = get_edges() if get_edges else None
            return state["edges"]

        def row_of(x, h):
            if 0 <= x < size_x:
                if step == 0:
                    return fin[s, h, pl.ds(x, F, stride=size_x), :]
                return buf_b[s, x, :, pl.ds(h * 128, 128)]
            edges = edges_of()
            if edges is None:
                return None
            return pick(edges[0], row_index + 32 * h + (64 if x > 0 else 0))

        def shift_part(i):
            span = range(chunk * i - 1, chunk * i + chunk + 1)
            rows = [[row_of(x, h) for h in range(2)] for x in span]
            state[i] = rows, shifted_sums(
                shift_f[...], jnp.concatenate([v for row in rows[1:-1] for v in row], axis=0)
            )

        def product_part(j):
            edges = edges_of()
            i, m = 2 * j // chunk, j % (chunk // 2)
            rows, shifted = state[i]
            if edges is None:
                ghost = 0.0
            else:
                ghost = jnp.where(edge_lane, pick(edges[1], col_index + 8 * j), 0.0)
            values = []
            for n in range(2):
                r = 2 * m + n + 1
                v0, v1 = rows[r]
                cross = [
                    jnp.where(lane >= 112, turn(v1, 112), ghost),
                    jnp.where(lane < 16, turn(v0, 16), ghost),
                ]
                for h in range(2):
                    at = F * (2 * (r - 1) + h)
                    part = shifted[at : at + F]
                    lateral = part[:, :128] + cross[h]
                    for near_row in (rows[r - 1][h], rows[r + 1][h]):
                        if near_row is not None:
                            lateral = lateral + near_row
                    values.append(keep_fine * rows[r][h] + kappa2 * lateral + part[:, 128:])
            state["p", j] = values, chemistry_product(wf_ref[...], values)

        def sum_part(j):
            values, product = state.pop(("p", j))
            rates = [
                wide(rate8[s, 2 * j + n, :, pl.ds(h * 128, 128)])
                for n in range(2) for h in range(2)
            ]
            new = chemistry_sum(product, values, rates, F)
            if step == 0:
                for n in range(2):
                    for h in range(2):
                        buf_b[s, 2 * j + n, :, pl.ds(h * 128, 128)] = new[2 * n + h]
            else:
                live = jnp.full((F, 128), parent_ref[s], jnp.int32) >= 0
                new = [jnp.where(live, v, 0.0) for v in new]
                for n in range(2):
                    for h in range(2):
                        fout[s, h, pl.ds(2 * j + n, F, stride=size_x), :] = new[2 * n + h]
                picked = []
                for h in range(2):
                    total = new[h] + new[2 + h]
                    total = total + turn(total, 127)
                    total = total + turn(total, 112)
                    picked.append(pick(total, mean_index))
                means[s, j] = 0.125 * jnp.where(mean_low, picked[0], picked[1])
            if done is not None:
                done(j)

        pairs = size_x // 2
        return [
            (
                functools.partial(shift_part, 2 * j // chunk) if 2 * j % chunk == 0 else None,
                functools.partial(product_part, j), functools.partial(sum_part, j),
            )
            for j in range(pairs)
        ]

    def run(jobs):
        lead, lag = 4, 2
        for n in range(-lead, len(jobs) + lag):
            if n + lead < len(jobs) and jobs[n + lead][0] is not None:
                jobs[n + lead][0]()
            if 0 <= n < len(jobs):
                jobs[n][1]()
            if n >= lag:
                jobs[n - lag][2]()

    def pack_edge_rate(s):
        for q in range(size_x // 4):
            total = jnp.zeros((8, 128), F32)
            for n in range(4):
                lo = turn(rate8[s, 4 * q + n, :, pl.ds(0, 128)], 16 * n)
                hi = turn(rate8[s, 4 * q + n, :, pl.ds(fine_cols - 128, 128)], 16 * n - 48)
                total = jnp.where(lane8 // 16 == n, lo, total)
                total = jnp.where(lane8 // 16 == 4 + n, hi, total)
            edge_rate[s, q] = total

    edge_index = (lane // 64) * 64 + ((lane % 64) // 32) * 8 + z16 // 2

    def correction(s):
        edge_x, edge_y = ring[0, s, 0], ring[0, s, 1]
        values, rates = [], []
        for side, x in ((0, 0), (1, last)):
            for h in range(2):
                values.append(kappa2 * pick(edge_x, row_index + 64 * side + 32 * h))
                rates.append(wide(rate8[s, x, :, pl.ds(h * 128, 128)]))
        for q in range(size_x // 4):
            values.append(kappa2 * pick(edge_y, edge_index + 16 * q))
            rates.append(wide(edge_rate[s, q]))
        return chemistry(wf_ref[...], values, rates, F)

    def correct(slot_list):
        shares = [correction(s) for s in slot_list]
        for s, share in zip(slot_list, shares):
            add_correction(s, share)

    def add_correction(s, share):
        for x in range(size_x):
            q, n = x // 4, x % 4
            both = share[4 + q]
            added = [
                jnp.where(lane < 16, turn(both, -16 * n), 0.0),
                jnp.where(lane >= 112, turn(both, 48 - 16 * n), 0.0),
            ]
            for h in range(2):
                if x == 0:
                    added[h] = added[h] + share[h]
                if x == last:
                    added[h] = added[h] + share[2 + h]
                here = (s, x, slice(None), pl.ds(h * 128, 128))
                buf_b[here] = buf_b[here] + added[h]

    def mid_edges(s):
        return [0.5 * (ring[0, s, side] + ring[1, s, side]) for side in range(2)]

    for s in order:
        for copy in fine_loads[s]:
            copy.wait()
    for s in order:
        spread_rate(s)
        pack_edge_rate(s)
    run([job for s in order for job in fine_jobs(s, 0, None)])

    homes = [jnp.full((F, 128), parent_ref[s], jnp.int32) for s in range(slots)]

    def fill_rows(rows):
        for at in range(0, len(rows), 4):
            tiles = [row_tile(x) for x in rows[at : at + 4]]
            result = react(coarse_tiles(tiles), [tile[5] for tile in tiles])
            for x, value in zip(rows[at : at + 4], result):
                cnew[x] = value

    fill_rows([x for x in range(1, last) if x not in (mid - 1, mid)])

    pl.semaphore_wait(ready_sem, 1 + len(sides))
    to_left = [send(1, send_l, rxr, (left, gy))]
    for n, y in enumerate(sides):
        to_left.append(send(6 + n, corner_send.at[0], rd.at[2 + n], (left, y)))

    for copy in to_right1:
        copy.wait_recv()
    tiles = [row_tile(-1), row_tile(0)]
    values = coarse_tiles(tiles)
    rates = [tile[5] for tile in tiles]
    values.append(
        kappa * extended(old_row(0), ry[0, near], turn(ry[1, near], 120))
    )
    rates.append(
        wide(
            extended(
                rxl[rate_rows], turn(corners[0][...], 40), turn(corners[1][...], 96), lane8
            )
        )
    )
    values.append(kappa * extended(rxl[near], tiles[0][3], tiles[0][4]))
    rates.append(
        wide(extended(crate_row(0), ry[0, rate_rows], turn(ry[1, rate_rows], 120), lane8))
    )
    result = react(values, rates)
    cnew[0] = result[1]
    for n, value in zip((4, 6, 8), (result[0], result[2], result[3])):
        cols_new[n] = value

    def far_rows():
        for copy in to_right2:
            copy.wait_recv()
        tiles = [
            (
                rx2[near], rx2[far], rxl[first_row],
                from_corner(corners2[0][...], 64, 0), from_corner(corners2[1][...], 0, 120), wide(rx2[rate_rows]),
            ),
        ]
        values = coarse_tiles(tiles)
        rates = [tile[5] for tile in tiles]
        values.append(kappa * extended(rx2[near], tiles[0][3], tiles[0][4]))
        rates.append(
            wide(
                extended(
                    rxl[first_rate], turn(corners[0][...], 32), turn(corners[1][...], 88), lane8
                )
            )
        )
        result = react(values, rates)
        cols_new[5] = result[0]
        cols_new[7] = result[1]

    def take_ring(level):
        before = cols_new[5] if level else rx2[near]
        after = cnew[0] if level else old_row(0)
        fix = end_shares(cols_new[7], cols_new[6]) if level else None
        shared = ring_recv[level, 0]
        turned = turn(shared, 64)
        for k in range(2):
            home = homes[k + 2]
            low, high = (shared, turned) if k == 0 else (turned, shared)
            kinds = [
                jnp.where(first_half, before, high), jnp.where(first_half, turn(before, 64), high),
                jnp.where(first_half, low, turn(after, 64)), jnp.where(first_half, low, after),
            ]
            value, added = kinds[3], fix[3] if level else None
            for p in range(3):
                value = jnp.where(home == p, kinds[p], value)
                if level:
                    added = jnp.where(home == p, fix[p], added)
            ring[level, k + 2, 0] = value
            value = ring_recv[level, 1 + k]
            ring[level, k + 2, 1] = value + added if level else value

    def local_rings():
        for copy in to_left:
            copy.wait_recv()
        tiles = [row_tile(last), row_tile(size_x)]
        values = coarse_tiles(tiles)
        values.append(
            kappa * extended(rxr[near], from_corner(corners[2][...], 64, 0), from_corner(corners[3][...], 0, 120))
        )
        rate = extended(crate_row(last), turn(ry[0, rate_rows], 8), ry[1, rate_rows], lane8)
        result = react(values, [tile[5] for tile in tiles] + [wide(rate)])
        cnew[last] = result[0]
        fix = end_shares(cols_new[8], result[2])
        tiles_old = ring_tiles(
            [rxl[near], old_row(mid - 1), old_row(mid), rxr[near]],
            [ry[0, near], cols[1], cols[2], ry[1, near]],
        )
        tiles_new = ring_tiles(
            [cols_new[4], cnew[mid - 1], cnew[mid], result[1]], [cols_new[n] for n in range(4)]
        )
        tiles_new = [(tile[0], tile[1] + fix[p]) for p, tile in enumerate(tiles_new)]
        for k in range(2):
            for side in range(2):
                ring[0, k, side] = chosen(tiles_old, k, side)
                ring[1, k, side] = chosen(tiles_new, k, side)

    def local_steps(slot_list):
        correct(slot_list)
        run(
            [
                job for s in slot_list
                for job in fine_jobs(s, 1, functools.partial(mid_edges, s))
            ]
        )

    @pl.when(gx == 0)
    def _():
        local_rings()
        local_steps((0,))

    far_rows()
    ring_old.wait_recv()
    take_ring(0)
    correct((2, 3))
    ring_new.wait_recv()
    take_ring(1)

    sent, jobs = [], []
    for s in (2, 3):
        def send_part(i, s=s):
            if 4 * (i + 1) % size_x:
                return
            i = 4 * i // size_x
            if s == 2 and i == 0:
                return
            for i in (0, 1) if s == 2 else (i,):
                send_half(i, s)

        def send_half(i, s):
            size = size_x // 8
            for m in range(size):
                j = 2 * (size * i + m)
                mean_send[s - 2, i, m] = jnp.where(first_half, means[s, j], means[s, j + 1])
            sent.append(
                send(
                    10 + 2 * (s - 2) + i, mean_send.at[s - 2, i], mean_recv.at[s - 2, i], (left, gy)
                )
            )

        jobs += fine_jobs(s, 1, functools.partial(mid_edges, s), send_part)
    run(jobs)

    @pl.when(gx == 0)
    def _():
        local_steps((1,))

    @pl.when(gx != 0)
    def _():
        local_rings()
        local_steps((0, 1))

    for copy in sent:
        copy.wait_recv()

    for x in range(size_x):
        a, X = x // mid, x % mid
        full = [means[0, X], means[1, X]]
        for k in range(2):
            packed = mean_recv[k, X // (mid // 2), (X % (mid // 2)) // 2]
            turned = turn(packed, 64)
            low, high = (packed, turned) if X % 2 == 0 else (turned, packed)
            full.append(jnp.where(first_half, low, high))
        owner = jnp.where(first_half, parents[2 * a], parents[2 * a + 1])
        value = cnew[x]
        for k in range(4):
            value = jnp.where(owner == k, full[k], value)
        cout[pl.ds(x, F, stride=size_x), :] = value
    for copy in to_right + to_side + to_left + [ring_old, ring_new] + sent:
        copy.wait_send()


def store_kernel(cout, fout, coarse_out_hbm, fine_out_hbm, sem):
    copies = [pltpu.make_async_copy(cout, coarse_out_hbm, sem.at[0])]
    slots = fout.shape[0]
    for s in range(slots):
        for h in range(2):
            copies.append(
                pltpu.make_async_copy(
                    fout.at[s, h], fine_out_hbm.at[s, :, pl.ds(h * 128, 128)],
                    sem.at[1 + 2 * s + h],
                )
            )
    for copy in copies:
        copy.start()
    for copy in copies:
        copy.wait()


def body(coarse_state, coarse_rate, fine_state, fine_rate, refine_to, parent_of, kappa, reaction):
    fields, size_x, merged = coarse_state.shape
    slots = fine_state.shape[0]
    fine_merged = fine_state.shape[3]
    flat = fields * size_x
    any_spec = pl.BlockSpec(memory_space=pl.ANY)
    vmem = pl.BlockSpec(memory_space=pltpu.VMEM)
    V = pltpu.VMEM
    tile = (fields, 128)
    cout, fout = pl.pallas_call(
        functools.partial(
            kernel, lax.axis_size("gx"), lax.axis_size("gy"), fields, size_x, slots
        ),
        out_shape=(V((flat, 128), F32), V((slots, 2, flat, 128), F32)),
        in_specs=[any_spec] * 8,
        out_specs=(vmem, vmem),
        scratch_shapes=[
            pltpu.SMEM((slots,), jnp.int32),
            pltpu.SMEM((slots,), jnp.int32),
            V((1, fields), F32),
            V((fields, fields), F32),
            V((flat, 128), F32),
            V((size_x, 128), F32),
            V((slots, 2, flat, 128), F32),
            V((slots, size_x, fine_merged), F32),
            V((slots, size_x, fields, fine_merged), F32),
            V((3 * fields + 16, 128), F32),
            V((2 * fields + 8, 128), F32),
            V((2, 2 * fields + 8, 128), F32),
            V((2, 8, 128), F32),
            V((3 * fields + 16, 128), F32),
            V((2 * fields + 8, 128), F32),
            V((2 * fields + 8, 128), F32),
            V((2, 2 * fields + 8, 128), F32),
            V((4, 8, 128), F32),
            V((2, 8, 128), F32),
            V((size_x,) + tile, F32),
            V((4,) + tile, F32),
            V((2, 8, 128), F32),
            V((2, slots, 2) + tile, F32),
            V((2, 3) + tile, F32),
            V((2, 3) + tile, F32),
            V((slots, size_x // 2) + tile, F32),
            V((2, 2, size_x // 8) + tile, F32),
            V((2, 2, size_x // 8) + tile, F32),
            V((9,) + tile, F32),
            V((4 * fields, 3 * fields), BF16),
            V((4 * fields, 3 * fields), BF16),
            V((slots, size_x, 8, fine_merged), F32),
            V((slots, size_x // 4, 8, 128), F32),
            V((256, 256), BF16),
            V((256, 256), BF16),
            pltpu.SemaphoreType.DMA((15,)),
            pltpu.SemaphoreType.DMA((17,)),
            pltpu.SemaphoreType.DMA((17,)),
            pltpu.SemaphoreType.REGULAR,
        ],
        compiler_params=pltpu.CompilerParams(
            collective_id=0, has_side_effects=True, vmem_limit_bytes=24 * 2**20
        ),
    )(
        *[
            pltpu.with_memory_space_constraint(array, pltpu.HBM)
            for array in (
                refine_to, parent_of, coarse_state.reshape(flat, merged), coarse_rate,
                fine_state.reshape(slots, flat, fine_merged), fine_rate,
                kappa.reshape(1, fields), reaction,
            )
        ]
    )
    coarse_out, fine_out = pl.pallas_call(
        store_kernel,
        out_shape=(
            jax.ShapeDtypeStruct((flat, merged), F32),
            jax.ShapeDtypeStruct((slots, flat, fine_merged), F32),
        ),
        in_specs=[vmem, vmem],
        out_specs=(any_spec, any_spec),
        scratch_shapes=[pltpu.SemaphoreType.DMA((1 + 2 * slots,))],
        compiler_params=pltpu.CompilerParams(vmem_limit_bytes=8 * 2**20),
    )(cout, fout)
    return coarse_out.reshape(coarse_state.shape), fine_out.reshape(fine_state.shape)


def solution(mesh):
    in_specs = (
        P(None, "gx", "gy"),
        P("gx", "gy"),
        P(("gx", "gy"), None, None, None),
        P(("gx", "gy"), None, None),
        P(("gx", "gy")),
        P(("gx", "gy")),
        P(),
        P(),
    )
    out_specs = (P(None, "gx", "gy"), P(("gx", "gy"), None, None, None))
    return jax.shard_map(body, mesh=mesh, in_specs=in_specs, out_specs=out_specs, check_vma=False)
```

```python
import functools
import jax
import jax.numpy as jnp
from jax import lax
from jax.experimental import pallas as pl
from jax.experimental.pallas import tpu as pltpu
from jax.sharding import PartitionSpec as P

MESH = pl.DeviceIdType.MESH
F32 = jnp.float32
BF16 = jnp.bfloat16


def lanes(rows):
    return lax.broadcasted_iota(jnp.int32, (rows, 128), 1)


def pick(table, index):
    return jnp.take_along_axis(table, index, axis=1)


def powers(reaction, fields):
    row = lax.broadcasted_iota(jnp.int32, (fields, 3 * fields), 0)
    col = lax.broadcasted_iota(jnp.int32, (fields, 3 * fields), 1)
    power = (col % fields == row).astype(F32)
    result = []
    for _ in range(4):
        power = jnp.dot(
            reaction, power, precision=lax.Precision.HIGHEST, preferred_element_type=F32
        )
        result.append(power)
    return result, col < 2 * fields


def chem_weights(power_list, high_part, step):
    parts = []
    for count, (choose, power) in enumerate(zip((4.0, 6.0, 4.0, 1.0), power_list)):
        value = power * (choose * step ** (count + 1))
        high = value.astype(BF16).astype(F32)
        parts.append(jnp.where(high_part, high, value - high))
    return jnp.concatenate(parts, axis=0).astype(BF16)


def chemistry_product(weights, values):
    wide = jnp.concatenate(values, axis=1)
    high = wide.astype(BF16).astype(F32)
    low = wide - high
    stacked = jnp.concatenate([high, low, high], axis=0).astype(BF16)
    return jnp.dot(weights, stacked, preferred_element_type=F32)


def chemistry_sum(product, values, rates, fields):
    out = []
    for n, (value, rate) in enumerate(zip(values, rates)):
        part = [
            product[q * fields : (q + 1) * fields, n * 128 : (n + 1) * 128] for q in range(4)
        ]
        rate = jnp.broadcast_to(rate, value.shape)
        out.append(value + rate * (part[0] + rate * (part[1] + rate * (part[2] + rate * part[3]))))
    return out


def chemistry(weights, values, rates, fields):
    return chemistry_sum(chemistry_product(weights, values), values, rates, fields)


def shift_matrix(group):
    row = lax.broadcasted_iota(jnp.int32, (256, 128), 0) % 128
    col = lax.broadcasted_iota(jnp.int32, (256, 128), 1)
    same = row // group == col // group
    lower = same & ((col - row + group) % group == 1)
    upper = same & ((row - col + group) % group == 1)
    side = (row - col == group) | (col - row == group)
    around = jnp.where(lower | upper | side, 1.0, 0.0)
    return jnp.concatenate([around, jnp.where(lower, 0.25, 0.0)], axis=1).astype(BF16)


def shifted_sums(matrix, rows):
    high = rows.astype(BF16)
    low = (rows - high.astype(F32)).astype(BF16)
    return jnp.dot(
        jnp.concatenate([high, low], axis=1), matrix, preferred_element_type=F32
    )


def turn(value, shift):
    shift = shift % 128
    return pltpu.roll(value, shift, 1) if shift else value


def kernel(
    n_gx, n_gy, fields, size_x, slots,
    refine_hbm, parent_hbm, coarse_hbm, crate_hbm, fine_hbm, frate_hbm, kappa_hbm, reaction_hbm,
    cout, fout,
    refine_ref, parent_ref, kappa_ref, reaction_ref, cin, crate, fin, frate, buf_b,
    send_r, send_l, col_send, corner_send, rxl, rxr, rx2, ry, rd, rd2, cnew, cols, rate_cols,
    ring, ring_send, ring_recv, means, mean_send, mean_recv,
    cols_new, wf_ref, wc_ref, rate8, edge_rate, shift_f, shift_c,
    in_sem, send_sem, recv_sem, ready_sem,
):
    F = fields
    fine_cols = frate.shape[2]
    last = size_x - 1
    mid = size_x // 2
    gx = lax.axis_index("gx")
    gy = lax.axis_index("gy")
    right = lax.rem(gx + 1, n_gx)
    left = lax.rem(gx + n_gx - 1, n_gx)
    above = lax.rem(gy + 1, n_gy)
    below = lax.rem(gy + n_gy - 1, n_gy)

    barrier = pltpu.get_barrier_semaphore()
    right2 = lax.rem(gx + 2, n_gx)
    left2 = lax.rem(gx + n_gx - 2, n_gx)
    sides = [above] if n_gy == 2 else [above, below]
    targets = [(x, y) for x in (left, left2) for y in [gy] + sides] + [(gx, y) for y in sides]
    for target in targets:
        pl.semaphore_signal(barrier, inc=1, device_id=target, device_id_type=MESH)

    load_coarse = pltpu.make_async_copy(coarse_hbm, cin, in_sem.at[0])
    load_crate = pltpu.make_async_copy(crate_hbm, crate, in_sem.at[1])
    load_frate = pltpu.make_async_copy(frate_hbm, frate, in_sem.at[2])
    fine_loads = [
        [
            pltpu.make_async_copy(
                fine_hbm.at[s, :, pl.ds(h * 128, 128)], fin.at[s, h], in_sem.at[3 + 2 * s + h]
            )
            for h in range(2)
        ]
        for s in range(slots)
    ]
    small = [
        pltpu.make_async_copy(reaction_hbm, reaction_ref, in_sem.at[11]),
        pltpu.make_async_copy(kappa_hbm, kappa_ref, in_sem.at[12]),
        pltpu.make_async_copy(refine_hbm, refine_ref, in_sem.at[13]),
        pltpu.make_async_copy(parent_hbm, parent_ref, in_sem.at[14]),
    ]
    order = (2, 3, 0, 1)
    for copy in [load_coarse, load_crate] + small + [load_frate]:
        copy.start()

    def send(n, src, dst, target):
        copy = pltpu.make_async_remote_copy(
            src_ref=src, dst_ref=dst, send_sem=send_sem.at[n], recv_sem=recv_sem.at[n],
            device_id=target, device_id_type=MESH,
        )
        copy.start()
        return copy

    lane = lanes(F)
    lane8 = lanes(8)
    first_half = lane < 64

    near, far, rate_rows = pl.ds(0, F), pl.ds(F, F), pl.ds(2 * F, 8)
    old_row = lambda x: cin[pl.ds(x, F, stride=size_x), :]
    crate_row = lambda x: jnp.broadcast_to(crate[pl.ds(x, 1), :], (8, 128))

    load_coarse.wait()
    load_crate.wait()
    for s in order:
        for copy in fine_loads[s]:
            copy.start()
    first_row, first_rate = pl.ds(2 * F + 8, F), pl.ds(3 * F + 8, 8)
    def fill_row_message(side, buf, x0, x1):
        row, rate = old_row(x0), crate_row(x0)
        buf[near] = row
        buf[far] = old_row(x1)
        buf[rate_rows] = rate
        pieces = [row[8 * j : 8 * j + 8] for j in range(F // 8)] + [rate]
        if side:
            buf[first_row] = old_row(0)
            buf[first_rate] = crate_row(0)
            pieces.append(crate_row(0))
        corner = pieces[0]
        for j, piece in enumerate(pieces):
            if j:
                corner = jnp.where(lane8 // 8 == j, turn(piece, 8 * j), corner)
            corner = jnp.where(lane8 // 8 == 8 + j, turn(piece, 8 * j - 56), corner)
        corner_send[side] = corner
    fill_row_message(1, send_r, last, last - 1)
    pl.semaphore_wait(barrier, len(targets))
    to_right = [
        send(0, send_r, rxl, (right, gy)),
        send(14, send_r.at[pl.ds(0, 2 * F + 8)], rx2, (right2, gy)),
    ]
    to_right1, to_right2 = to_right[:1], to_right[1:]
    for n, y in enumerate(sides):
        to_right1.append(send(4 + n, corner_send.at[1], rd.at[n], (right, y)))
        to_right2.append(send(15 + n, corner_send.at[1], rd2.at[n], (right2, y)))
    to_right = to_right1 + to_right2
    for y in [gy] + sides:
        pl.semaphore_signal(ready_sem, inc=1, device_id=(right, y), device_id_type=MESH)

    group32 = lanes(F + 8) // 8
    columns = {
        x: jnp.concatenate([old_row(x), crate_row(x)], axis=0) for x in range(size_x)
    }
    wanted = (0, 1, mid - 2, mid - 1, mid, mid + 1, last - 1, last)
    bits = [size_x // 8, size_x // 4, 1, size_x // 2]
    for n, bit in enumerate(bits):
        free = sum(bits[n + 1 :])
        moved = {}
        for x in range(size_x):
            if any((x ^ y) & ~free == 0 for y in wanted):
                other = columns[x ^ bit]
                lower = group32 & bit == 0
                if x & bit:
                    moved[x] = jnp.where(lower, turn(other, -8 * bit), columns[x])
                else:
                    moved[x] = jnp.where(lower, columns[x], turn(other, 8 * bit))
        columns = moved
    for side, (y0, y1) in enumerate(((0, 1), (last, last - 1))):
        col_send[side, near] = columns[y0][:F]
        col_send[side, far] = columns[y1][:F]
        col_send[side, rate_rows] = columns[y0][F:]
    to_side = [
        send(2, col_send.at[1], ry.at[0], (gx, above)),
        send(3, col_send.at[0], ry.at[1], (gx, below)),
    ]
    for n in range(4):
        cols[n] = columns[mid - 2 + n][:F]
    for n in range(2):
        rate_cols[n] = columns[mid - 1 + n][F:]

    for copy in small:
        copy.wait()
    power_list, high_part = powers(reaction_ref[...], F)
    wf_ref[...] = chem_weights(power_list, high_part, 0.125)
    wc_ref[...] = chem_weights(power_list, high_part, 0.25)
    diag = lax.broadcasted_iota(jnp.int32, (F, F), 0) == lax.broadcasted_iota(jnp.int32, (F, F), 1)
    kappa_col = jnp.sum(
        jnp.where(diag, jnp.broadcast_to(kappa_ref[...], (F, F)), 0.0), axis=1, keepdims=True
    )
    kappa = jnp.broadcast_to(kappa_col, (F, 128))
    kappa2 = 2.0 * kappa
    keep_fine = 0.75 - 6.0 * kappa2
    keep_coarse = 0.75 - 6.0 * kappa
    shift_c[...] = shift_matrix(8)
    fill_row_message(0, send_l, 0, 1)
    corners = [rd.at[n] for n in ((0, 0, 2, 2) if n_gy == 2 else (0, 1, 2, 3))]
    corners2 = [rd2.at[n] for n in ((0, 0) if n_gy == 2 else (0, 1))]

    def wide(rate):
        return jnp.concatenate([rate] * (F // 8), axis=0)

    def from_corner(tile, src, dst):
        return jnp.concatenate([turn(tile, dst - src - 8 * j) for j in range(F // 8)], axis=0)

    def coarse_tiles(tiles):
        centers = jnp.concatenate([tile[0] for tile in tiles], axis=0)
        shifted = shifted_sums(shift_c[...], centers)
        values = []
        for n, (center, lo, hi, ghost_lo, ghost_hi, _) in enumerate(tiles):
            part = shifted[F * n : F * n + F]
            lateral = (lo + hi) + part[:, :128]
            if ghost_lo is not None:
                edge = jnp.where(lane >= 120, ghost_hi, 0.0)
                lateral = lateral + jnp.where(lane < 8, ghost_lo, edge)
            values.append(keep_coarse * center + kappa * lateral + part[:, 128:])
        return values

    def react(values, rates):
        out = []
        for at in range(0, len(values), 4):
            out += chemistry(wc_ref[...], values[at : at + 4], rates[at : at + 4], F)
        return out

    def row_tile(x):
        if x == -1:
            return (
                rxl[near], rxl[far], old_row(0),
                from_corner(corners[0][...], 64, 0), from_corner(corners[1][...], 0, 120), wide(rxl[rate_rows]),
            )
        if x == size_x:
            return (
                rxr[near], old_row(last), rxr[far],
                from_corner(corners[2][...], 64, 0), from_corner(corners[3][...], 0, 120), wide(rxr[rate_rows]),
            )
        return (
            old_row(x),
            old_row(x - 1) if x else rxl[near],
            old_row(x + 1) if x < last else rxr[near],
            turn(ry[0, near], -8 * x), turn(ry[1, near], 120 - 8 * x),
            crate[pl.ds(x, 1), :],
        )

    def extended(row, lo, hi, at=None):
        at = lane if at is None else at
        return jnp.where(at < 8, lo, jnp.where(at >= 120, hi, row))

    def joined(lo, hi, half):
        if half == 0:
            return jnp.where(first_half, lo, turn(hi, 64))
        return jnp.where(first_half, turn(lo, 64), hi)

    parents = [jnp.full((F, 128), refine_ref[p], jnp.int32) for p in range(4)]

    def ring_tiles(row_at, col_at):
        return [
            (
                joined(row_at[p // 2], row_at[p // 2 + 2], p % 2),
                joined(col_at[p % 2], col_at[p % 2 + 2], p // 2),
            )
            for p in range(4)
        ]

    def chosen(tiles, k, side):
        value = jnp.zeros((F, 128), F32)
        for p in range(4):
            value = jnp.where(parents[p] == k, tiles[p][side], value)
        return value

    def send_ring(level, low_row, high_row, col_at):
        tiles = ring_tiles([low_row] * 4, col_at)
        halves = []
        for k in range(2):
            value = jnp.zeros((F, 128), F32)
            for p in range(4):
                row = low_row if p // 2 else high_row
                row = row if p % 2 == k else turn(row, 64)
                value = jnp.where(parents[p] == k + 2, row, value)
            halves.append(value)
            ring_send[level, 1 + k] = chosen(tiles, k + 2, 1)
        ring_send[level, 0] = jnp.where(first_half, halves[0], halves[1])
        return send(8 + level, ring_send.at[level], ring_recv.at[level], (right, gy))

    group = lane // 8

    def end_shares(before, after):
        at_first = (group == 0) | (group == 8)
        at_last = (group == 7) | (group == 15)
        return [
            jnp.where(at_first, before, 0.0), jnp.where(at_first, turn(before, 72), 0.0),
            jnp.where(at_last, turn(after, 56), 0.0), jnp.where(at_last, after, 0.0),
        ]

    for copy in to_side:
        copy.wait_recv()
    old_cols = [ry[0, near], cols[1], cols[2], ry[1, near]]
    ring_old = send_ring(0, old_row(mid - 1), old_row(mid), old_cols)
    tiles = [
        row_tile(mid - 1), row_tile(mid),
        (ry[0, near], ry[0, far], col_send[0, near], None, None, wide(ry[0, rate_rows])),
        (cols[1], cols[0], cols[2], None, None, wide(rate_cols[0])),
        (cols[2], cols[1], cols[3], None, None, wide(rate_cols[1])),
        (ry[1, near], col_send[1, near], ry[1, far], None, None, wide(ry[1, rate_rows])),
    ]
    result = react(coarse_tiles(tiles), [tile[5] for tile in tiles])
    cnew[mid - 1], cnew[mid] = result[:2]
    for n in range(4):
        cols_new[n] = result[2 + n]
    ring_new = send_ring(1, result[0], result[1], result[2:])

    shift_f[...] = shift_matrix(16)
    z16 = lane % 16
    row_index = (lane // 32) * 8 + z16 // 2
    col_index = jnp.where(lane < 64, 0, 64) + z16 // 2
    target = lane % 64
    mean_index = ((target // 8) % 4) * 32 + 2 * (target % 8)
    mean_low = target // 32 == 0
    edge_lane = (lane < 16) | (lane >= 112)

    load_frate.wait()

    chunk = 8

    def spread_rate(s):
        for x in range(size_x):
            rate8[s, x] = jnp.broadcast_to(frate[s, pl.ds(x, 1), :], rate8.shape[2:])

    def fine_jobs(s, step, get_edges, done=None):
        state = {}

        def edges_of():
            if "edges" not in state:
                state["edges"] = get_edges() if get_edges else None
            return state["edges"]

        def row_of(x, h):
            if 0 <= x < size_x:
                if step == 0:
                    return fin[s, h, pl.ds(x, F, stride=size_x), :]
                return buf_b[s, x, :, pl.ds(h * 128, 128)]
            edges = edges_of()
            if edges is None:
                return None
            return pick(edges[0], row_index + 32 * h + (64 if x > 0 else 0))

        def shift_part(i):
            span = range(chunk * i - 1, chunk * i + chunk + 1)
            rows = [[row_of(x, h) for h in range(2)] for x in span]
            state[i] = rows, shifted_sums(
                shift_f[...], jnp.concatenate([v for row in rows[1:-1] for v in row], axis=0)
            )

        def product_part(j):
            edges = edges_of()
            i, m = 2 * j // chunk, j % (chunk // 2)
            rows, shifted = state[i]
            if edges is None:
                ghost = 0.0
            else:
                ghost = jnp.where(edge_lane, pick(edges[1], col_index + 8 * j), 0.0)
            values = []
            for n in range(2):
                r = 2 * m + n + 1
                v0, v1 = rows[r]
                cross = [
                    jnp.where(lane >= 112, turn(v1, 112), ghost),
                    jnp.where(lane < 16, turn(v0, 16), ghost),
                ]
                for h in range(2):
                    at = F * (2 * (r - 1) + h)
                    part = shifted[at : at + F]
                    lateral = part[:, :128] + cross[h]
                    for near_row in (rows[r - 1][h], rows[r + 1][h]):
                        if near_row is not None:
                            lateral = lateral + near_row
                    values.append(keep_fine * rows[r][h] + kappa2 * lateral + part[:, 128:])
            state["p", j] = values, chemistry_product(wf_ref[...], values)

        def sum_part(j):
            values, product = state.pop(("p", j))
            rates = [
                wide(rate8[s, 2 * j + n, :, pl.ds(h * 128, 128)])
                for n in range(2) for h in range(2)
            ]
            new = chemistry_sum(product, values, rates, F)
            if step == 0:
                for n in range(2):
                    for h in range(2):
                        buf_b[s, 2 * j + n, :, pl.ds(h * 128, 128)] = new[2 * n + h]
            else:
                live = jnp.full((F, 128), parent_ref[s], jnp.int32) >= 0
                new = [jnp.where(live, v, 0.0) for v in new]
                for n in range(2):
                    for h in range(2):
                        fout[s, h, pl.ds(2 * j + n, F, stride=size_x), :] = new[2 * n + h]
                picked = []
                for h in range(2):
                    total = new[h] + new[2 + h]
                    total = total + turn(total, 127)
                    total = total + turn(total, 112)
                    picked.append(pick(total, mean_index))
                means[s, j] = 0.125 * jnp.where(mean_low, picked[0], picked[1])
            if done is not None:
                done(j)

        pairs = size_x // 2
        return [
            (
                functools.partial(shift_part, 2 * j // chunk) if 2 * j % chunk == 0 else None,
                functools.partial(product_part, j), functools.partial(sum_part, j),
            )
            for j in range(pairs)
        ]

    def run(jobs):
        lead, lag = 4, 2
        for n in range(-lead, len(jobs) + lag):
            if n + lead < len(jobs) and jobs[n + lead][0] is not None:
                jobs[n + lead][0]()
            if 0 <= n < len(jobs):
                jobs[n][1]()
            if n >= lag:
                jobs[n - lag][2]()

    def pack_edge_rate(s):
        for q in range(size_x // 4):
            total = jnp.zeros((8, 128), F32)
            for n in range(4):
                lo = turn(rate8[s, 4 * q + n, :, pl.ds(0, 128)], 16 * n)
                hi = turn(rate8[s, 4 * q + n, :, pl.ds(fine_cols - 128, 128)], 16 * n - 48)
                total = jnp.where(lane8 // 16 == n, lo, total)
                total = jnp.where(lane8 // 16 == 4 + n, hi, total)
            edge_rate[s, q] = total

    edge_index = (lane // 64) * 64 + ((lane % 64) // 32) * 8 + z16 // 2

    def correction(s):
        edge_x, edge_y = ring[0, s, 0], ring[0, s, 1]
        values, rates = [], []
        for side, x in ((0, 0), (1, last)):
            for h in range(2):
                values.append(kappa2 * pick(edge_x, row_index + 64 * side + 32 * h))
                rates.append(wide(rate8[s, x, :, pl.ds(h * 128, 128)]))
        for q in range(size_x // 4):
            values.append(kappa2 * pick(edge_y, edge_index + 16 * q))
            rates.append(wide(edge_rate[s, q]))
        return chemistry(wf_ref[...], values, rates, F)

    def correct(slot_list):
        shares = [correction(s) for s in slot_list]
        for s, share in zip(slot_list, shares):
            add_correction(s, share)

    def add_correction(s, share):
        for x in range(size_x):
            q, n = x // 4, x % 4
            both = share[4 + q]
            added = [
                jnp.where(lane < 16, turn(both, -16 * n), 0.0),
                jnp.where(lane >= 112, turn(both, 48 - 16 * n), 0.0),
            ]
            for h in range(2):
                if x == 0:
                    added[h] = added[h] + share[h]
                if x == last:
                    added[h] = added[h] + share[2 + h]
                here = (s, x, slice(None), pl.ds(h * 128, 128))
                buf_b[here] = buf_b[here] + added[h]

    def mid_edges(s):
        return [0.5 * (ring[0, s, side] + ring[1, s, side]) for side in range(2)]

    for s in order:
        for copy in fine_loads[s]:
            copy.wait()
    for s in order:
        spread_rate(s)
        pack_edge_rate(s)
    run([job for s in order for job in fine_jobs(s, 0, None)])

    homes = [jnp.full((F, 128), parent_ref[s], jnp.int32) for s in range(slots)]

    def fill_rows(rows):
        for at in range(0, len(rows), 4):
            tiles = [row_tile(x) for x in rows[at : at + 4]]
            result = react(coarse_tiles(tiles), [tile[5] for tile in tiles])
            for x, value in zip(rows[at : at + 4], result):
                cnew[x] = value

    fill_rows([x for x in range(1, last) if x not in (mid - 1, mid)])

    pl.semaphore_wait(ready_sem, 1 + len(sides))
    to_left = [send(1, send_l, rxr, (left, gy))]
    for n, y in enumerate(sides):
        to_left.append(send(6 + n, corner_send.at[0], rd.at[2 + n], (left, y)))

    for copy in to_right1:
        copy.wait_recv()
    tiles = [row_tile(-1), row_tile(0)]
    values = coarse_tiles(tiles)
    rates = [tile[5] for tile in tiles]
    values.append(
        kappa * extended(old_row(0), ry[0, near], turn(ry[1, near], 120))
    )
    rates.append(
        wide(
            extended(
                rxl[rate_rows], turn(corners[0][...], 40), turn(corners[1][...], 96), lane8
            )
        )
    )
    values.append(kappa * extended(rxl[near], tiles[0][3], tiles[0][4]))
    rates.append(
        wide(extended(crate_row(0), ry[0, rate_rows], turn(ry[1, rate_rows], 120), lane8))
    )
    result = react(values, rates)
    cnew[0] = result[1]
    for n, value in zip((4, 6, 8), (result[0], result[2], result[3])):
        cols_new[n] = value

    def far_rows():
        for copy in to_right2:
            copy.wait_recv()
        tiles = [
            (
                rx2[near], rx2[far], rxl[first_row],
                from_corner(corners2[0][...], 64, 0), from_corner(corners2[1][...], 0, 120), wide(rx2[rate_rows]),
            ),
        ]
        values = coarse_tiles(tiles)
        rates = [tile[5] for tile in tiles]
        values.append(kappa * extended(rx2[near], tiles[0][3], tiles[0][4]))
        rates.append(
            wide(
                extended(
                    rxl[first_rate], turn(corners[0][...], 32), turn(corners[1][...], 88), lane8
                )
            )
        )
        result = react(values, rates)
        cols_new[5] = result[0]
        cols_new[7] = result[1]

    def take_ring(level):
        before = cols_new[5] if level else rx2[near]
        after = cnew[0] if level else old_row(0)
        fix = end_shares(cols_new[7], cols_new[6]) if level else None
        shared = ring_recv[level, 0]
        turned = turn(shared, 64)
        for k in range(2):
            home = homes[k + 2]
            low, high = (shared, turned) if k == 0 else (turned, shared)
            kinds = [
                jnp.where(first_half, before, high), jnp.where(first_half, turn(before, 64), high),
                jnp.where(first_half, low, turn(after, 64)), jnp.where(first_half, low, after),
            ]
            value, added = kinds[3], fix[3] if level else None
            for p in range(3):
                value = jnp.where(home == p, kinds[p], value)
                if level:
                    added = jnp.where(home == p, fix[p], added)
            ring[level, k + 2, 0] = value
            value = ring_recv[level, 1 + k]
            ring[level, k + 2, 1] = value + added if level else value

    def local_rings():
        for copy in to_left:
            copy.wait_recv()
        tiles = [row_tile(last), row_tile(size_x)]
        values = coarse_tiles(tiles)
        values.append(
            kappa * extended(rxr[near], from_corner(corners[2][...], 64, 0), from_corner(corners[3][...], 0, 120))
        )
        rate = extended(crate_row(last), turn(ry[0, rate_rows], 8), ry[1, rate_rows], lane8)
        result = react(values, [tile[5] for tile in tiles] + [wide(rate)])
        cnew[last] = result[0]
        fix = end_shares(cols_new[8], result[2])
        tiles_old = ring_tiles(
            [rxl[near], old_row(mid - 1), old_row(mid), rxr[near]],
            [ry[0, near], cols[1], cols[2], ry[1, near]],
        )
        tiles_new = ring_tiles(
            [cols_new[4], cnew[mid - 1], cnew[mid], result[1]], [cols_new[n] for n in range(4)]
        )
        tiles_new = [(tile[0], tile[1] + fix[p]) for p, tile in enumerate(tiles_new)]
        for k in range(2):
            for side in range(2):
                ring[0, k, side] = chosen(tiles_old, k, side)
                ring[1, k, side] = chosen(tiles_new, k, side)

    def local_steps(slot_list):
        run(
            [
                job for s in slot_list
                for job in fine_jobs(s, 1, functools.partial(mid_edges, s))
            ]
        )

    @pl.when(gx == 0)
    def _():
        local_rings()
        correct((0, 1))

    far_rows()
    ring_old.wait_recv()
    take_ring(0)
    correct((2, 3))
    ring_new.wait_recv()
    take_ring(1)

    sent, jobs = [], []
    for s in (2, 3):
        def send_part(i, s=s):
            if 4 * (i + 1) % size_x:
                return
            i = 4 * i // size_x
            if s == 2 and i == 0:
                return
            for i in (0, 1) if s == 2 else (i,):
                send_half(i, s)

        def send_half(i, s):
            size = size_x // 8
            for m in range(size):
                j = 2 * (size * i + m)
                mean_send[s - 2, i, m] = jnp.where(first_half, means[s, j], means[s, j + 1])
            sent.append(
                send(
                    10 + 2 * (s - 2) + i, mean_send.at[s - 2, i], mean_recv.at[s - 2, i], (left, gy)
                )
            )

        jobs += fine_jobs(s, 1, functools.partial(mid_edges, s), send_part)
    run(jobs)

    @pl.when(gx != 0)
    def _():
        local_rings()
        correct((0, 1))

    local_steps((0, 1))

    for copy in sent:
        copy.wait_recv()

    for x in range(size_x):
        a, X = x // mid, x % mid
        full = [means[0, X], means[1, X]]
        for k in range(2):
            packed = mean_recv[k, X // (mid // 2), (X % (mid // 2)) // 2]
            turned = turn(packed, 64)
            low, high = (packed, turned) if X % 2 == 0 else (turned, packed)
            full.append(jnp.where(first_half, low, high))
        owner = jnp.where(first_half, parents[2 * a], parents[2 * a + 1])
        value = cnew[x]
        for k in range(4):
            value = jnp.where(owner == k, full[k], value)
        cout[pl.ds(x, F, stride=size_x), :] = value
    for copy in to_right + to_side + to_left + [ring_old, ring_new] + sent:
        copy.wait_send()


def store_kernel(cout, fout, coarse_out_hbm, fine_out_hbm, sem):
    copies = [pltpu.make_async_copy(cout, coarse_out_hbm, sem.at[0])]
    slots = fout.shape[0]
    for s in range(slots):
        for h in range(2):
            copies.append(
                pltpu.make_async_copy(
                    fout.at[s, h], fine_out_hbm.at[s, :, pl.ds(h * 128, 128)],
                    sem.at[1 + 2 * s + h],
                )
            )
    for copy in copies:
        copy.start()
    for copy in copies:
        copy.wait()


def body(coarse_state, coarse_rate, fine_state, fine_rate, refine_to, parent_of, kappa, reaction):
    fields, size_x, merged = coarse_state.shape
    slots = fine_state.shape[0]
    fine_merged = fine_state.shape[3]
    flat = fields * size_x
    any_spec = pl.BlockSpec(memory_space=pl.ANY)
    vmem = pl.BlockSpec(memory_space=pltpu.VMEM)
    V = pltpu.VMEM
    tile = (fields, 128)
    cout, fout = pl.pallas_call(
        functools.partial(
            kernel, lax.axis_size("gx"), lax.axis_size("gy"), fields, size_x, slots
        ),
        out_shape=(V((flat, 128), F32), V((slots, 2, flat, 128), F32)),
        in_specs=[any_spec] * 8,
        out_specs=(vmem, vmem),
        scratch_shapes=[
            pltpu.SMEM((slots,), jnp.int32),
            pltpu.SMEM((slots,), jnp.int32),
            V((1, fields), F32),
            V((fields, fields), F32),
            V((flat, 128), F32),
            V((size_x, 128), F32),
            V((slots, 2, flat, 128), F32),
            V((slots, size_x, fine_merged), F32),
            V((slots, size_x, fields, fine_merged), F32),
            V((3 * fields + 16, 128), F32),
            V((2 * fields + 8, 128), F32),
            V((2, 2 * fields + 8, 128), F32),
            V((2, 8, 128), F32),
            V((3 * fields + 16, 128), F32),
            V((2 * fields + 8, 128), F32),
            V((2 * fields + 8, 128), F32),
            V((2, 2 * fields + 8, 128), F32),
            V((4, 8, 128), F32),
            V((2, 8, 128), F32),
            V((size_x,) + tile, F32),
            V((4,) + tile, F32),
            V((2, 8, 128), F32),
            V((2, slots, 2) + tile, F32),
            V((2, 3) + tile, F32),
            V((2, 3) + tile, F32),
            V((slots, size_x // 2) + tile, F32),
            V((2, 2, size_x // 8) + tile, F32),
            V((2, 2, size_x // 8) + tile, F32),
            V((9,) + tile, F32),
            V((4 * fields, 3 * fields), BF16),
            V((4 * fields, 3 * fields), BF16),
            V((slots, size_x, 8, fine_merged), F32),
            V((slots, size_x // 4, 8, 128), F32),
            V((256, 256), BF16),
            V((256, 256), BF16),
            pltpu.SemaphoreType.DMA((15,)),
            pltpu.SemaphoreType.DMA((17,)),
            pltpu.SemaphoreType.DMA((17,)),
            pltpu.SemaphoreType.REGULAR,
        ],
        compiler_params=pltpu.CompilerParams(
            collective_id=0, has_side_effects=True, vmem_limit_bytes=24 * 2**20
        ),
    )(
        *[
            pltpu.with_memory_space_constraint(array, pltpu.HBM)
            for array in (
                refine_to, parent_of, coarse_state.reshape(flat, merged), coarse_rate,
                fine_state.reshape(slots, flat, fine_merged), fine_rate,
                kappa.reshape(1, fields), reaction,
            )
        ]
    )
    coarse_out, fine_out = pl.pallas_call(
        store_kernel,
        out_shape=(
            jax.ShapeDtypeStruct((flat, merged), F32),
            jax.ShapeDtypeStruct((slots, flat, fine_merged), F32),
        ),
        in_specs=[vmem, vmem],
        out_specs=(any_spec, any_spec),
        scratch_shapes=[pltpu.SemaphoreType.DMA((1 + 2 * slots,))],
        compiler_params=pltpu.CompilerParams(vmem_limit_bytes=8 * 2**20),
    )(cout, fout)
    return coarse_out.reshape(coarse_state.shape), fine_out.reshape(fine_state.shape)


def solution(mesh):
    in_specs = (
        P(None, "gx", "gy"),
        P("gx", "gy"),
        P(("gx", "gy"), None, None, None),
        P(("gx", "gy"), None, None),
        P(("gx", "gy")),
        P(("gx", "gy")),
        P(),
        P(),
    )
    out_specs = (P(None, "gx", "gy"), P(("gx", "gy"), None, None, None))
    return jax.shard_map(body, mesh=mesh, in_specs=in_specs, out_specs=out_specs, check_vma=False)
```
